512 devices in a mesh: row: 32 (over x, z_lo, core), col: 16 (over z_hi, y).
Axes of the slice: x: 4, y: 8, z: 8 (z_hi: 2, z_lo: 4; z = z_hi * 4 + z_lo), core: 2. Of those that a mesh axis runs over, the one named last changes fastest.
Arguments:
- cached_inverse: float32 [4, 32, 128, 8, 16, 128], P(None, 'row', None, None, 'col'), may hold values from -6 to 6
- parent_panel: float32 [256, 96, 128], P('col', 'row'), may hold values from -0.046875 to 0.046875
- parent_blocks: int32 [96], P('row'), may hold values from -1 to 127, as said below
- parent_sizes: int32 [96], P('row'), may hold values from 0 to 128, as said below
- parent_diagonal: float32 [256, 256], P('col'), may hold values from -6 to 6
- child_panel: float32 [256, 96, 128], P('col', 'row'), may hold values from -0.046875 to 0.046875
- child_top: float32 [256, 256], P('col'), may hold values from -0.375 to 0.375
- child_blocks: int32 [96], P('row'), may hold values from -1 to 127, as said below
- child_sizes: int32 [96], P('row'), may hold values from 0 to 128, as said below
- child_diagonal: float32 [256, 256], P('col'), may hold values from -6 to 6
Outputs:
- parent_rows: float32 [4, 32, 128, 256], P(None, 'row', 'col')
- parent_diag: float32 [256, 256], P('col')
- child_rows: float32 [4, 32, 128, 256], P(None, 'row', 'col')
- child_upper: float32 [256, 256], P('col')
- child_diag: float32 [256, 256], P('col')
The draws below stay inside these ranges and needn't reach their ends.
Inputs may be any that keep to these rules, and one draw needn't show every extreme that they name: `parent_blocks`: slots p*3 to p*3 + 2 belong to index p of row; their live slots come first, name distinct block numbers congruent to p modulo the size of row, and the rest hold -1. Some index of row has 3 live slots. `parent_sizes`: 0 exactly for the slots that hold -1 in parent_blocks. `child_blocks`: slot k holds either parent_blocks[k] (a live parent slot) or -1. `child_sizes`: 0 exactly for the slots that hold -1 in child_blocks, else at most parent_sizes of the same slot.
All inputs are finite; a program needn't handle non-finite values.
Results may differ from the reference program's by a relative error of at most 0.000096.
Values sent between devices are 32-bit elements; how exact they have to be, the bound alone decides.
A program may use at most 64 MiB of HBM per device.

```python
import jax
import jax.numpy as jnp
from jax import lax

W = 256
B = 128
RC = 4
RPD = 3
NB = 128
M = 16384
CC = 8
SLOTS = 96
N_ROW = 32
N_COL = 16


def structure(key):
    rows_total = NB // RC
    key_list = jax.random.split(jax.random.fold_in(key, 11), 5)
    counts = jax.random.randint(key_list[0], (rows_total,), 1, RPD + 1)
    counts = counts.at[0].set(RPD).at[1].set(1)
    scores = jax.random.randint(key_list[1], (rows_total, RC), 0, 1 << 20) * RC + jnp.arange(RC, dtype=jnp.int32)[None, :]
    scores = scores.at[rows_total - 1, RC - 1].set(-1)
    ranking = jnp.argsort(scores, axis=1, stable=True)[:, :RPD].astype(jnp.int32)
    slot_index = jnp.arange(RPD, dtype=jnp.int32)
    is_live = slot_index[None, :] < counts[:, None]
    owner_row = jnp.arange(rows_total, dtype=jnp.int32)[:, None]
    blocks = jnp.where(is_live, ranking * rows_total + owner_row, -1)
    block_sizes = jnp.where(is_live, jax.random.randint(key_list[2], (rows_total, RPD), 1, B + 1), 0)
    block_sizes = block_sizes.at[0, 0].set(B)
    retained = jax.random.randint(key_list[3], (rows_total, RPD), 0, 5) < 3
    retained = retained.at[0, 0].set(True).at[rows_total - 1, 0].set(True)
    child_live = is_live & retained
    child_blocks = jnp.where(child_live, blocks, -1)
    child_sizes = jnp.where(child_live, jax.random.randint(key_list[4], (rows_total, RPD), 1, jnp.maximum(block_sizes, 1) + 1), 0)
    child_sizes = child_sizes.at[0, 0].set(B)
    return (blocks.reshape(-1).astype(jnp.int32), block_sizes.reshape(-1).astype(jnp.int32), child_blocks.reshape(-1).astype(jnp.int32), child_sizes.reshape(-1).astype(jnp.int32))


def draw_parent_blocks(key, part):
    return structure(key)[0]


def draw_parent_sizes(key, part):
    return structure(key)[1]


def draw_child_blocks(key, part):
    return structure(key)[2]


def draw_child_sizes(key, part):
    return structure(key)[3]


def block_scale(rng, shape, cuts, smallest, top_value):
    loudness, own = 1.0, jax.random.fold_in(rng, 6)
    for axis_at, blocks in cuts:
        draws = jnp.exp(jax.random.uniform(jax.random.fold_in(own, axis_at), (blocks,), jnp.float32, smallest / len(cuts), top_value / len(cuts)))
        loudness = loudness * jnp.repeat(draws, shape[axis_at] // blocks).reshape([-1 if axis == axis_at else 1 for axis in range(len(shape))])
    return loudness


def gaussian(own_key, extent, width, limit, cuts=(), kind=jnp.bfloat16):
    result = width * jax.random.normal(own_key, extent, jnp.float32)
    if cuts:
        result = result * block_scale(own_key, extent, cuts, -0.22, 0.18)
    return jnp.clip(result, -limit, limit).astype(kind)


def setup_inputs(seed: int = 0) -> dict:
    arg_keys = jax.random.split(jax.random.key(seed), 11)
    return {
        "cached_inverse": gaussian(arg_keys[0], (RC, N_ROW, B, CC, N_COL, B), 1.0, 6.0, ((1, 32), (4, 16)), jnp.float32),
        "parent_panel": gaussian(arg_keys[1], (W, SLOTS, B), M ** -0.5, 0.046875, ((0, 16), (1, 32)), jnp.float32),
        "parent_blocks": draw_parent_blocks(jax.random.fold_in(arg_keys[10], 71), 0),
        "parent_sizes": draw_parent_sizes(jax.random.fold_in(arg_keys[10], 71), 0),
        "parent_diagonal": gaussian(arg_keys[4], (W, W), 1.0, 6.0, ((0, 16),), jnp.float32),
        "child_panel": gaussian(arg_keys[5], (W, SLOTS, B), M ** -0.5, 0.046875, ((0, 16), (1, 32)), jnp.float32),
        "child_top": gaussian(arg_keys[6], (W, W), W ** -0.5, 0.375, ((0, 16),), jnp.float32),
        "child_blocks": draw_child_blocks(jax.random.fold_in(arg_keys[10], 71), 0),
        "child_sizes": draw_child_sizes(jax.random.fold_in(arg_keys[10], 71), 0),
        "child_diagonal": gaussian(arg_keys[9], (W, W), 1.0, 6.0, ((0, 16),), jnp.float32),
    }


highest = lax.Precision.HIGHEST


def dense_panel(panel, blocks, sizes):
    row_live = (jnp.arange(B, dtype=jnp.int32)[None, :] < sizes[:, None]).astype(jnp.float32)
    onehot = (blocks[None, :] == jnp.arange(NB, dtype=jnp.int32)[:, None]).astype(jnp.float32)
    masked = panel * row_live[None, :, :]
    dense = jnp.einsum("nk,wkb->nbw", onehot, masked, precision=highest).reshape(M, W)
    row_mask = jnp.einsum("nk,kb->nb", onehot, row_live, precision=highest).reshape(M)
    return dense, row_mask


def reference(cached_inverse, parent_panel, parent_blocks, parent_sizes, parent_diagonal, child_panel, child_top, child_blocks, child_sizes, child_diagonal):
    matrix = cached_inverse.reshape(M, M)
    parent_dense, parent_mask = dense_panel(parent_panel, parent_blocks, parent_sizes)
    parent_rows = -jnp.dot(matrix, parent_dense, precision=highest, preferred_element_type=jnp.float32) * parent_mask[:, None]
    parent_diag = parent_diagonal - jnp.dot(parent_dense.T, parent_rows, precision=highest, preferred_element_type=jnp.float32)
    child_dense, child_mask = dense_panel(child_panel, child_blocks, child_sizes)
    child_rows = -(jnp.dot(matrix, child_dense, precision=highest, preferred_element_type=jnp.float32) + jnp.dot(parent_rows, child_top, precision=highest, preferred_element_type=jnp.float32)) * child_mask[:, None]
    child_upper = -(jnp.dot(parent_diag, child_top, precision=highest, preferred_element_type=jnp.float32) + jnp.dot(parent_rows.T, child_dense, precision=highest, preferred_element_type=jnp.float32))
    child_diag = child_diagonal - jnp.dot(child_top.T, child_upper, precision=highest, preferred_element_type=jnp.float32) - jnp.dot(child_dense.T, child_rows, precision=highest, preferred_element_type=jnp.float32)
    return (parent_rows.reshape(RC, N_ROW, B, W), parent_diag, child_rows.reshape(RC, N_ROW, B, W), child_upper, child_diag)
```

```python
import jax
import jax.numpy as jnp
from jax import lax
from jax.experimental import pallas as pl
from jax.experimental.pallas import tpu as pltpu
from jax.sharding import PartitionSpec as P

MESH = pl.DeviceIdType.MESH
F32 = jnp.float32
BF16 = jnp.bfloat16

NX, NZL, NZH, NY, NK = 4, 4, 2, 8, 2
NZ = NZL * NZH
NROW, NCOL = NX * NZL * NK, NZH * NY
W, B, SL, RC = 256, 128, 3, 4
SHARE = W // NCOL
ROWS = SL * B
CB = B // NCOL
PATCH = 2 * ROWS + 128
OWN = W + 2 * ROWS


def place():
    p = lax.axis_index("row")
    q = lax.axis_index("col")
    x = p // (NZL * NK)
    zl = (p // NK) % NZL
    k = p % NK
    return p, q, x, zl, k, q // NY, q % NY


def row_id(x, zl, k):
    return (x * NZL + zl) * NK + k


def rcopy(src, dst, send, recv, target):
    return pltpu.make_async_remote_copy(
        src_ref=src,
        dst_ref=dst,
        send_sem=send,
        recv_sem=recv,
        device_id=target,
        device_id_type=MESH,
    )


def spread_kernel(
    x_ref, g_ref, c_ref, ps, pr, lsem, zs, zr, xs, xr, ks, kr, hs, hr, us, ur, ds, dr
):
    p, q, x, zl, k, zh, y = place()
    half, cls = p // NCOL, p % NCOL
    fixed = q == cls
    swap = (half * NCOL + q, cls)
    core = (row_id(x, zl, 1 - k), q)
    zdev = [None] + [(row_id(x, (zl + d) % NZL, k), q) for d in range(1, NZL)]
    xdev = [None] + [(row_id((x + d) % NX, zl, k), q) for d in range(1, NX)]
    hdev = (p, (1 - zh) * NY + y)
    up = (p, zh * NY + (y + 1) % NY)
    down = (p, zh * NY + (y + NY - 1) % NY)

    barrier = pltpu.get_barrier_semaphore()
    for dev in zdev[1:] + xdev[1:] + [core, hdev, up, down]:
        pl.semaphore_signal(barrier, inc=1, device_id=dev, device_id_type=MESH)

    @pl.when(jnp.logical_not(fixed))
    def _():
        pl.semaphore_signal(barrier, inc=1, device_id=swap, device_id_type=MESH)

    pl.semaphore_wait(barrier, NZL - 1 + NX - 1 + 4 + jnp.where(fixed, 0, 1))

    sends = []

    def send(*args):
        copy = rcopy(*args)
        copy.start()
        sends.append(copy)

    piece = x_ref.at[:, W : W + PATCH]
    mine = x_ref.at[:, 0:OWN]

    out = rcopy(piece, g_ref.at[half * NCOL + q], ps.at[0], pr.at[0], swap)
    local = pltpu.make_async_copy(piece, g_ref.at[p], lsem.at[0])

    @pl.when(jnp.logical_not(fixed))
    def _():
        out.start()

    @pl.when(fixed)
    def _():
        local.start()

    def ring(a, t, src_up, src_down):
        zz = zh if a == 0 else 1 - zh
        if src_up is not None:
            at = zz * NY + (y + NY - t) % NY
            send(src_up, c_ref.at[at], us.at[a * 4 + t], ur.at[a * 4 + t], up)
        if src_down is not None:
            at = zz * NY + (y + t) % NY
            send(src_down, c_ref.at[at], ds.at[a * 3 + t], dr.at[a * 3 + t], down)

    def ring_up_wait(a, t):
        zz = zh if a == 0 else 1 - zh
        got = c_ref.at[zz * NY + (y + NY - 1 - t) % NY]
        rcopy(got, got, us.at[a * 4 + t], ur.at[a * 4 + t], up).wait_recv()
        if t < 3:
            ring(a, t + 1, got, None)

    def ring_down_wait(a, t):
        zz = zh if a == 0 else 1 - zh
        got = c_ref.at[zz * NY + (y + 1 + t) % NY]
        rcopy(got, got, ds.at[a * 3 + t], dr.at[a * 3 + t], down).wait_recv()
        if t < 2:
            ring(a, t + 1, None, got)

    send(mine, c_ref.at[q], hs.at[0], hr.at[0], hdev)
    ring(0, 0, mine, mine)
    c_ref[q] = x_ref[:, 0:OWN]

    ring_up_wait(0, 0)
    ring_down_wait(0, 0)
    other = c_ref.at[(1 - zh) * NY + y]
    rcopy(other, other, hs.at[0], hr.at[0], hdev).wait_recv()
    ring(1, 0, other, other)

    @pl.when(jnp.logical_not(fixed))
    def _():
        rcopy(piece, g_ref.at[p], ps.at[0], pr.at[0], swap).wait_recv()

    @pl.when(fixed)
    def _():
        local.wait()

    def fan(src, dz):
        got = g_ref.at[src]
        for d in range(1, NX):
            send(got, got, xs.at[dz * 3 + d - 1], xr.at[dz * 3 + d - 1], xdev[d])
        send(got, got, ks.at[dz * 4], kr.at[dz * 4], core)

    own = g_ref.at[p]
    for d in range(1, NZL):
        send(own, own, zs.at[d - 1], zr.at[d - 1], zdev[d])
    fan(p, 0)

    def z_wait(d):
        src = row_id(x, (zl + NZL - d) % NZL, k)
        got = g_ref.at[src]
        rcopy(got, got, zs.at[d - 1], zr.at[d - 1], zdev[d]).wait_recv()
        fan(src, d)

    def x_wait(dz, d):
        src = row_id((x + NX - d) % NX, (zl + NZL - dz) % NZL, k)
        got = g_ref.at[src]
        rcopy(got, got, xs.at[dz * 3 + d - 1], xr.at[dz * 3 + d - 1], xdev[d]).wait_recv()
        send(got, got, ks.at[dz * 4 + d], kr.at[dz * 4 + d], core)

    ring_up_wait(0, 1)
    ring_down_wait(0, 1)
    ring_up_wait(1, 0)
    ring_down_wait(1, 0)
    z_wait(1)
    z_wait(3)
    ring_up_wait(0, 2)
    ring_up_wait(1, 1)
    ring_down_wait(1, 1)
    z_wait(2)
    for d in (1, 3, 2):
        x_wait(0, d)
    ring_up_wait(1, 2)
    for dz in (1, 3, 2):
        for d in (1, 3, 2):
            x_wait(dz, d)
    ring_down_wait(0, 2)
    ring_up_wait(0, 3)
    ring_down_wait(1, 2)
    ring_up_wait(1, 3)
    for dz in range(NZL):
        for d in range(NX):
            src = row_id((x + NX - d) % NX, (zl + NZL - dz) % NZL, 1 - k)
            got = g_ref.at[src]
            rcopy(got, got, ks.at[dz * 4 + d], kr.at[dz * 4 + d], core).wait_recv()

    @pl.when(jnp.logical_not(fixed))
    def _():
        out.wait_send()

    for copy in sends:
        copy.wait_send()


def spread(pieces):
    vmem = pl.BlockSpec(memory_space=pltpu.VMEM)
    dma = pltpu.SemaphoreType.DMA
    return pl.pallas_call(
        spread_kernel,
        out_shape=(
            jax.ShapeDtypeStruct((NROW, SHARE, PATCH), F32),
            jax.ShapeDtypeStruct((NCOL, SHARE, OWN), F32),
        ),
        in_specs=[vmem],
        out_specs=(vmem, vmem),
        scratch_shapes=[
            dma((1,)), dma((1,)), dma((1,)),
            dma((3,)), dma((3,)),
            dma((12,)), dma((12,)),
            dma((16,)), dma((16,)),
            dma((1,)), dma((1,)),
            dma((8,)), dma((8,)),
            dma((6,)), dma((6,)),
        ],
        compiler_params=pltpu.CompilerParams(collective_id=0, has_side_effects=True),
        name="spread",
    )(pieces)


def halves(a):
    hi = a.astype(BF16)
    lo = (a - hi.astype(F32)).astype(BF16)
    return hi, lo


def dot3(a, b, dims):
    def one(u, v):
        return lax.dot_general(u, v, (dims, ((), ())), preferred_element_type=F32)

    return one(a[0], b[0]) + (one(a[0], b[1]) + one(a[1], b[0]))


NN = ((1,), (0,))
NT = ((1,), (1,))


def multiply_kernel(idx, s_ref, g_ref, c_ref, d_ref, yz_ref, aue_ref, sub, yv, zv, uv):
    for s in range(SL):
        for t in range(2 * SL):
            start = idx[s] * (B * 8) + idx[SL + t]
            sub[s * B : (s + 1) * B, t * B : (t + 1) * B] = s_ref[pl.ds(start, B, stride=8), :]
    gp = [halves(g_ref[h, :, 0:ROWS]) for h in range(2)]
    gq = [halves(g_ref[h, :, ROWS : 2 * ROWS]) for h in range(2)]
    top = halves(c_ref[:, 0:W])
    rows = lax.broadcasted_iota(jnp.int32, (B, 1), 0)
    for s in range(SL):
        at = slice(s * B, (s + 1) * B)
        left = [halves(sub[at, h * ROWS : (h + 1) * ROWS]) for h in range(2)]
        yp = dot3(left[0], gp[0], NT) + dot3(left[1], gp[1], NT)
        y = jnp.where(rows < idx[9 + s], -yp, 0.0)
        zq = dot3(left[0], gq[0], NT) + dot3(left[1], gq[1], NT)
        z = jnp.where(rows < idx[12 + s], -(zq + dot3(halves(y), top, NN)), 0.0)
        yv[at, :] = y
        zv[at, :] = z
        yz_ref[:, s * CB : (s + 1) * CB, 0:W] = y.reshape(NCOL, CB, W)
        yz_ref[:, s * CB : (s + 1) * CB, W : 2 * W] = z.reshape(NCOL, CB, W)
    pp = halves(c_ref[:, W : W + ROWS])
    qp = halves(c_ref[:, W + ROWS : OWN])
    y = halves(yv[...])
    a = dot3(pp, y, NN)
    uv[...] = dot3(halves(a), top, NN) - dot3(qp, y, NN).T

    @pl.when(idx[16] == 1)
    def _():
        own = pl.ds(pl.multiple_of(idx[15], SHARE), SHARE)
        uv[own, :] = uv[own, :] - dot3(halves(d_ref[...]), top, NN)

    u = uv[...]
    e = -dot3(halves(c_ref[:, 0:W].T), halves(u), NN) - dot3(qp, halves(zv[...]), NN)
    for m, mat in enumerate((a, u, e)):
        for k in range(2):
            aue_ref[k, m] = mat[:, k * 128 : (k + 1) * 128]


def multiply(idx, s, g, c, d):
    vmem = pl.BlockSpec(memory_space=pltpu.VMEM)
    return pl.pallas_call(
        multiply_kernel,
        out_shape=(
            jax.ShapeDtypeStruct((NCOL, SL * CB, 2 * W), F32),
            jax.ShapeDtypeStruct((2, 3, W, 128), F32),
        ),
        in_specs=[pl.BlockSpec(memory_space=pltpu.SMEM), vmem, vmem, vmem, vmem],
        out_specs=(vmem, vmem),
        scratch_shapes=[
            pltpu.VMEM((ROWS, 2 * ROWS), F32),
            pltpu.VMEM((ROWS, W), F32),
            pltpu.VMEM((ROWS, W), F32),
            pltpu.VMEM((W, W), F32),
        ],
        name="multiply",
    )(idx, s, g, c, d)


def gather_kernel(
    yz_ref, aue_ref, yzo, auo,
    kbuf, acc, xbuf, accx, ybuf, accy, zbuf, yzbuf, yzacc, hbuf,
    ks, kr, xs, xr, ys, yr, zs, zr, fs, fr, vs, vr, hs, hr,
):
    p, q, x, zl, k, zh, y = place()
    z = zh * NZL + zl
    xk = {}
    for d in range(NX):
        for f in range(2):
            if d or f:
                xk[d, f] = (row_id((x + d) % NX, zl, k if f == 0 else 1 - k), q)
    ydev = [None] + [(p, zh * NY + (y + d) % NY) for d in range(1, NY)]
    zpos = [(z + d) % NZ for d in range(NZ)]
    zdev = [None] + [(row_id(x, zpos[d] % NZL, k), (zpos[d] // NZL) * NY + y) for d in range(1, NZ)]

    barrier = pltpu.get_barrier_semaphore()
    for dev in list(xk.values()) + ydev[1:] + zdev[1:]:
        pl.semaphore_signal(barrier, inc=1, device_id=dev, device_id_type=MESH)
    pl.semaphore_wait(barrier, 7 + NY - 1 + NZ - 1)

    core = rcopy(aue_ref.at[1 - k], kbuf, ks.at[0], kr.at[0], xk[0, 1])
    core.start()
    ycopies = []
    for d in (1, 7, 2, 6, 3, 5, 4):
        copy = rcopy(
            yz_ref.at[:, (y + d) % NY], yzbuf.at[d - 1], vs.at[d - 1], vr.at[d - 1], ydev[d]
        )
        copy.start()
        ycopies.append(copy)

    core.wait_recv()
    acc[...] = aue_ref[k] + kbuf[...]
    busy = x < 3

    def xsend(d):
        m = (x + d) % NX
        return m, lambda: rcopy(
            acc.at[m], xbuf.at[d - 1], xs.at[d - 1], xr.at[d - 1], xk[d, 0]
        )

    for d in (2, 1, 3):
        m, make = xsend(d)

        @pl.when(m < 3)
        def _():
            make().start()

    @pl.when(busy)
    def _():
        for d in range(1, NX):
            got = xbuf.at[d - 1]
            rcopy(got, got, xs.at[d - 1], xr.at[d - 1], xk[d, 0]).wait_recv()
        total = (acc[x] + xbuf[0]) + (xbuf[1] + xbuf[2])
        accx[...] = total.reshape(NZH, NY, SHARE, 128)
        for d in range(1, NY):
            rcopy(
                accx.at[:, (y + d) % NY], ybuf.at[d - 1], ys.at[d - 1], yr.at[d - 1], ydev[d]
            ).start()
        for d in range(1, NY):
            got = ybuf.at[d - 1]
            rcopy(got, got, ys.at[d - 1], yr.at[d - 1], ydev[d]).wait_recv()
        total = accx[:, y]
        for d in range(NY - 1):
            total = total + ybuf[d]
        accy[...] = total
        for d in range(1, NZ):
            rcopy(
                accy.at[zpos[d] // NZL], zbuf.at[d - 1], zs.at[d - 1], zr.at[d - 1], zdev[d]
            ).start()

    for copy in ycopies:
        copy.wait_recv()
    total = yz_ref[:, y]
    for d in range(NY - 1):
        total = total + yzbuf[d]
    yzacc[...] = total
    hop = rcopy(yzacc.at[1 - zh], hbuf, hs.at[0], hr.at[0], zdev[NZL])
    hop.start()

    def fsend(d, f):
        n = d * 2 + f - 1
        return rcopy(auo.at[x, k], auo.at[x, k], fs.at[n], fr.at[n], xk[d, f])

    @pl.when(busy)
    def _():
        for d in range(1, NZ):
            got = zbuf.at[d - 1]
            rcopy(got, got, zs.at[d - 1], zr.at[d - 1], zdev[d]).wait_recv()
        total = accy[zh]
        for d in range(NZ - 1):
            total = total + zbuf[d]
        auo[x, k] = total
        for d, f in xk:
            fsend(d, f).start()

    hop.wait_recv()
    yzo[...] = yzacc[zh] + hbuf[...]

    for d, f in xk:
        m = (x + NX - d) % NX
        n = d * 2 + f - 1

        @pl.when(m < 3)
        def _():
            got = auo.at[m, k if f == 0 else 1 - k]
            rcopy(got, got, fs.at[n], fr.at[n], xk[d, f]).wait_recv()

    core.wait_send()
    hop.wait_send()
    for copy in ycopies:
        copy.wait_send()
    for d in (2, 1, 3):
        m, make = xsend(d)

        @pl.when(m < 3)
        def _():
            make().wait_send()

    @pl.when(busy)
    def _():
        for d in range(1, NY):
            rcopy(
                accx.at[:, (y + d) % NY], ybuf.at[d - 1], ys.at[d - 1], yr.at[d - 1], ydev[d]
            ).wait_send()
        for d in range(1, NZ):
            rcopy(
                accy.at[zpos[d] // NZL], zbuf.at[d - 1], zs.at[d - 1], zr.at[d - 1], zdev[d]
            ).wait_send()
        for d, f in xk:
            fsend(d, f).wait_send()


def gather(yz, aue):
    vmem = pl.BlockSpec(memory_space=pltpu.VMEM)
    dma = pltpu.SemaphoreType.DMA
    rows = SL * CB
    return pl.pallas_call(
        gather_kernel,
        out_shape=(
            jax.ShapeDtypeStruct((rows, 2 * W), F32),
            jax.ShapeDtypeStruct((3, 2, SHARE, 128), F32),
        ),
        in_specs=[vmem, vmem],
        out_specs=(vmem, vmem),
        scratch_shapes=[
            pltpu.VMEM((3, W, 128), F32),
            pltpu.VMEM((3, W, 128), F32),
            pltpu.VMEM((3, W, 128), F32),
            pltpu.VMEM((NZH, NY, SHARE, 128), F32),
            pltpu.VMEM((NY - 1, NZH, SHARE, 128), F32),
            pltpu.VMEM((NZH, SHARE, 128), F32),
            pltpu.VMEM((NZ - 1, SHARE, 128), F32),
            pltpu.VMEM((NY - 1, NZH, rows, 2 * W), F32),
            pltpu.VMEM((NZH, rows, 2 * W), F32),
            pltpu.VMEM((rows, 2 * W), F32),
            dma((1,)), dma((1,)),
            dma((3,)), dma((3,)),
            dma((7,)), dma((7,)),
            dma((7,)), dma((7,)),
            dma((7,)), dma((7,)),
            dma((7,)), dma((7,)),
            dma((1,)), dma((1,)),
        ],
        compiler_params=pltpu.CompilerParams(collective_id=1, has_side_effects=True),
        name="gather",
    )(yz, aue)


def body(
    cached_inverse,
    parent_panel,
    parent_blocks,
    parent_sizes,
    parent_diagonal,
    child_panel,
    child_top,
    child_blocks,
    child_sizes,
    child_diagonal,
):
    row_index = lax.axis_index("row")
    col_index = lax.axis_index("col")
    lane = jnp.arange(B, dtype=jnp.int32)[None, :]
    parent_live = lane < parent_sizes[:, None]
    child_live = lane < child_sizes[:, None]
    parent_own = jnp.where(parent_live[None], parent_panel, 0.0).reshape(SHARE, ROWS)
    child_own = jnp.where(child_live[None], child_panel, 0.0).reshape(SHARE, ROWS)
    local = jnp.maximum(parent_blocks, 0) // NROW
    tags = jnp.broadcast_to(jnp.pad(local.astype(F32), (0, 128 - SL))[None], (SHARE, 128))
    pieces = jnp.concatenate([child_top, parent_own, child_own, tags], axis=1)
    patch, own = spread(pieces)
    heard = patch[:: NCOL, 0, 2 * ROWS : 2 * ROWS + SL].astype(jnp.int32)
    columns = heard * 2 + jnp.arange(2, dtype=jnp.int32)[:, None]
    idx = jnp.concatenate([
        local,
        columns.reshape(-1),
        parent_sizes,
        child_sizes,
        jnp.stack([col_index * SHARE, (row_index == 0).astype(jnp.int32)]),
    ])
    yz, aue = multiply(
        idx,
        cached_inverse.reshape(RC * B * 8, B),
        patch.reshape(2, W, PATCH),
        own.reshape(W, OWN),
        parent_diagonal,
    )
    rows, mats = gather(yz.reshape(NZH, NY, SL * CB, 2 * W), aue)
    put = (parent_blocks[None, :] == (jnp.arange(RC, dtype=jnp.int32) * NROW + row_index)[:, None])
    rows = rows.reshape(SL, CB, 2 * W)
    laid = sum(jnp.where(put[:, s][:, None, None], rows[s][None], 0.0) for s in range(SL))
    mats = jnp.transpose(mats, (0, 2, 1, 3)).reshape(3, SHARE, W)
    return (
        laid[:, None, :, 0:W],
        parent_diagonal - mats[0],
        laid[:, None, :, W:],
        mats[1],
        child_diagonal + mats[2],
    )


def solution(mesh):
    in_specs = (
        P(None, "row", None, None, "col", None),
        P("col", "row", None),
        P("row"),
        P("row"),
        P("col", None),
        P("col", "row", None),
        P("col", None),
        P("row"),
        P("row"),
        P("col", None),
    )
    out_specs = (
        P(None, "row", "col", None),
        P("col", None),
        P(None, "row", "col", None),
        P("col", None),
        P("col", None),
    )
    return jax.shard_map(body, mesh=mesh, in_specs=in_specs, out_specs=out_specs, check_vma=False)
```

```python
import jax
import jax.numpy as jnp
from jax import lax
from jax.experimental import pallas as pl
from jax.experimental.pallas import tpu as pltpu
from jax.sharding import PartitionSpec as P

MESH = pl.DeviceIdType.MESH
F32 = jnp.float32
BF16 = jnp.bfloat16

NX, NZL, NZH, NY, NK = 4, 4, 2, 8, 2
NZ = NZL * NZH
NROW, NCOL = NX * NZL * NK, NZH * NY
W, B, SL, RC = 256, 128, 3, 4
SHARE = W // NCOL
ROWS = SL * B
CB = B // NCOL
PATCH = 2 * ROWS + 128
OWN = W + 2 * ROWS
WIDE = W + PATCH
UPS = (4, 3)
DOWNS = (3, 4)


def place():
    p = lax.axis_index("row")
    q = lax.axis_index("col")
    x = p // (NZL * NK)
    zl = (p // NK) % NZL
    k = p % NK
    return p, q, x, zl, k, q // NY, q % NY


def row_id(x, zl, k):
    return (x * NZL + zl) * NK + k


def rcopy(src, dst, send, recv, target):
    return pltpu.make_async_remote_copy(
        src_ref=src,
        dst_ref=dst,
        send_sem=send,
        recv_sem=recv,
        device_id=target,
        device_id_type=MESH,
    )


def halves(a):
    hi = a.astype(BF16)
    lo = (a - hi.astype(F32)).astype(BF16)
    return hi, lo


def dot3(a, b, dims):
    def one(u, v):
        return lax.dot_general(u, v, (dims, ((), ())), preferred_element_type=F32)

    return one(a[0], b[0]) + (one(a[0], b[1]) + one(a[1], b[0]))


NN = ((1,), (0,))
NT = ((1,), (1,))


def pick(values, which, first=0):
    out = values[0]
    for n in range(1, len(values)):
        out = jnp.where(which == n, values[n], out)
    return out


def step_kernel(
    pb, psz, csz, s_hbm, pp_ref, cp_ref, top_ref, d_ref,
    yzo, auo,
    sv, sub8, sub, xv, g_ref, c_ref, yv, zv, uv, yz, aue,
    kbuf, acc, xbuf, accx, ybuf, accy, zbuf, ubuf, dbuf, yzacc, hbuf,
    ssem, ps, pr, lsem, gzs, gzr, gxs, gxr, gks, gkr, chs, chr_, cus, cur, cds, cdr,
    ks, kr, xs, xr, ys, yr, zs, zr, fs, fr, us, ur, ds, dr, hs, hr,
):
    p, q, x, zl, k, zh, y = place()
    z = zh * NZL + zl
    half, cls = p // NCOL, p % NCOL
    fixed = q == cls
    swap = (half * NCOL + q, cls)
    xk = {}
    for d in range(NX):
        for f in range(2):
            if d or f:
                xk[d, f] = (row_id((x + d) % NX, zl, k if f == 0 else 1 - k), q)
    core = xk[0, 1]
    lzdev = [None] + [(row_id(x, (zl + d) % NZL, k), q) for d in range(1, NZL)]
    ydev = [None] + [(p, zh * NY + (y + d) % NY) for d in range(1, NY)]
    up, down = ydev[1], ydev[NY - 1]
    zpos = [(z + d) % NZ for d in range(NZ)]
    zdev = [None] + [(row_id(x, zpos[d] % NZL, k), (zpos[d] // NZL) * NY + y) for d in range(1, NZ)]
    far = zdev[NZL]

    load_s = pltpu.make_async_copy(s_hbm, sv, ssem.at[0])
    load_s.start()

    barrier = pltpu.get_barrier_semaphore()

    @pl.when(jnp.logical_not(fixed))
    def _():
        pl.semaphore_signal(barrier, inc=1, device_id=swap, device_id_type=MESH)

    for dev in zdev[1:] + ydev[1:] + list(xk.values()):
        pl.semaphore_signal(barrier, inc=1, device_id=dev, device_id_type=MESH)

    lane = lax.broadcasted_iota(jnp.int32, (SHARE, B), 1)
    xv[:, 0:W] = top_ref[...]
    for s in range(SL):
        at = W + s * B
        xv[:, at : at + B] = jnp.where(lane < psz[s], pp_ref[s], 0.0)
        at += ROWS
        xv[:, at : at + B] = jnp.where(lane < csz[s], cp_ref[s], 0.0)
    local = [jnp.maximum(pb[s], 0) // NROW for s in range(SL)]
    tag = jnp.zeros((SHARE, 128), F32)
    tags = lax.broadcasted_iota(jnp.int32, (SHARE, 128), 1)
    for s in range(SL):
        tag = jnp.where(tags == s, local[s].astype(F32), tag)
    xv[:, OWN:WIDE] = tag
    c_ref[q] = xv[:, 0:OWN]

    pl.semaphore_wait(barrier, 7 + NY - 1 + NZ - 1 + jnp.where(fixed, 0, 1))

    sends = []

    def send(*args):
        copy = rcopy(*args)
        copy.start()
        sends.append(copy)

    piece = xv.at[:, W:WIDE]
    mine = xv.at[:, 0:OWN]
    out = rcopy(piece, g_ref.at[half * NCOL + q], ps.at[0], pr.at[0], swap)
    keep = pltpu.make_async_copy(piece, g_ref.at[p], lsem.at[0])

    @pl.when(jnp.logical_not(fixed))
    def _():
        out.start()

    @pl.when(fixed)
    def _():
        keep.start()

    def ring(a, t, src_up, src_down):
        zz = zh if a == 0 else 1 - zh
        if src_up is not None:
            at = zz * NY + (y + NY - t) % NY
            send(src_up, c_ref.at[at], cus.at[a * 4 + t], cur.at[a * 4 + t], up)
        if src_down is not None:
            at = zz * NY + (y + t) % NY
            send(src_down, c_ref.at[at], cds.at[a * 4 + t], cdr.at[a * 4 + t], down)

    def ring_up_wait(a, t):
        zz = zh if a == 0 else 1 - zh
        got = c_ref.at[zz * NY + (y + NY - 1 - t) % NY]
        rcopy(got, got, cus.at[a * 4 + t], cur.at[a * 4 + t], up).wait_recv()
        if t + 1 < UPS[a]:
            ring(a, t + 1, got, None)

    def ring_down_wait(a, t):
        zz = zh if a == 0 else 1 - zh
        got = c_ref.at[zz * NY + (y + 1 + t) % NY]
        rcopy(got, got, cds.at[a * 4 + t], cdr.at[a * 4 + t], down).wait_recv()
        if t + 1 < DOWNS[a]:
            ring(a, t + 1, None, got)

    send(mine, c_ref.at[q], chs.at[0], chr_.at[0], far)
    ring(0, 0, mine, mine)

    load_s.wait()
    for s in range(SL):
        for c in range(8):
            blocks = [sv[pl.ds(r * B * 8 + c, B, stride=8), :] for r in range(RC)]
            sub8[s * B : (s + 1) * B, c * B : (c + 1) * B] = pick(blocks, local[s])

    ring_up_wait(0, 0)
    ring_down_wait(0, 0)
    other = c_ref.at[(1 - zh) * NY + y]
    rcopy(other, other, chs.at[0], chr_.at[0], far).wait_recv()
    ring(1, 0, other, other)

    @pl.when(jnp.logical_not(fixed))
    def _():
        rcopy(piece, g_ref.at[p], ps.at[0], pr.at[0], swap).wait_recv()

    @pl.when(fixed)
    def _():
        keep.wait()

    def fan(src, dz):
        got = g_ref.at[src]
        for d in (1, 3):
            send(got, got, gxs.at[dz * 3 + d - 1], gxr.at[dz * 3 + d - 1], xk[d, 0])
        send(got, got, gks.at[dz * 4], gkr.at[dz * 4], core)

    own = g_ref.at[p]
    for d in (1, 3, 2):
        send(own, own, gzs.at[d - 1], gzr.at[d - 1], lzdev[d])
    fan(p, 0)

    def z_wait(d):
        src = row_id(x, (zl + NZL - d) % NZL, k)
        got = g_ref.at[src]
        rcopy(got, got, gzs.at[d - 1], gzr.at[d - 1], lzdev[d]).wait_recv()
        fan(src, d)

    def x_wait(dz, d):
        src = row_id((x + NX - d) % NX, (zl + NZL - dz) % NZL, k)
        got = g_ref.at[src]
        n = dz * 3 + d - 1
        rcopy(got, got, gxs.at[n], gxr.at[n], xk[d, 0]).wait_recv()
        n = dz * 3 + 1
        if d == (1 if dz % 2 == 0 else 3):
            send(got, got, gxs.at[n], gxr.at[n], xk[d, 0])
        send(got, got, gks.at[dz * 4 + d], gkr.at[dz * 4 + d], core)

    ring_up_wait(0, 1)
    ring_down_wait(0, 1)
    ring_up_wait(1, 0)
    ring_down_wait(1, 0)
    z_wait(1)
    z_wait(3)
    x_wait(0, 1)
    x_wait(0, 3)
    ring_up_wait(0, 2)
    ring_up_wait(1, 1)
    ring_down_wait(1, 1)
    z_wait(2)
    x_wait(1, 1)
    x_wait(1, 3)
    x_wait(3, 1)
    x_wait(3, 3)
    ring_down_wait(0, 2)
    ring_up_wait(0, 3)
    ring_up_wait(1, 2)
    ring_down_wait(1, 2)
    x_wait(0, 2)
    x_wait(2, 1)
    x_wait(2, 3)
    x_wait(1, 2)
    x_wait(3, 2)
    ring_down_wait(1, 3)
    x_wait(2, 2)
    for dz in (0, 1, 3, 2):
        for d in (0, 1, 3, 2):
            src = row_id((x + NX - d) % NX, (zl + NZL - dz) % NZL, 1 - k)
            got = g_ref.at[src]
            rcopy(got, got, gks.at[dz * 4 + d], gkr.at[dz * 4 + d], core).wait_recv()

    for h in range(2):
        heard = g_ref[h * NCOL, 0:8, 2 * ROWS : 2 * ROWS + 128]
        for t in range(SL):
            which = jnp.max(jnp.where(tags[0:8] == t, heard, 0.0))
            for s in range(SL):
                at = slice(s * B, (s + 1) * B)
                blocks = [sub8[at, (2 * r + h) * B : (2 * r + h + 1) * B] for r in range(RC)]
                n = h * SL + t
                value = blocks[0]
                for r in range(1, RC):
                    value = jnp.where(which > r - 0.5, blocks[r], value)
                sub[at, n * B : (n + 1) * B] = value

    def panel(h, at):
        return halves(g_ref[h * NCOL : (h + 1) * NCOL, :, at : at + ROWS].reshape(W, ROWS))

    gp = [panel(h, 0) for h in range(2)]
    gq = [panel(h, ROWS) for h in range(2)]
    topf = c_ref[:, :, 0:W].reshape(W, W)
    top = halves(topf)
    rows = lax.broadcasted_iota(jnp.int32, (B, 1), 0)
    for s in range(SL):
        at = slice(s * B, (s + 1) * B)
        left = [halves(sub[at, h * ROWS : (h + 1) * ROWS]) for h in range(2)]
        yp = dot3(left[0], gp[0], NT) + dot3(left[1], gp[1], NT)
        yy = jnp.where(rows < psz[s], -yp, 0.0)
        zq = dot3(left[0], gq[0], NT) + dot3(left[1], gq[1], NT)
        zz = jnp.where(rows < csz[s], -(zq + dot3(halves(yy), top, NN)), 0.0)
        yv[at, :] = yy
        zv[at, :] = zz
        yz[:, :, s * CB : (s + 1) * CB, 0:W] = yy.reshape(NZH, NY, CB, W)
        yz[:, :, s * CB : (s + 1) * CB, W : 2 * W] = zz.reshape(NZH, NY, CB, W)

    def sum_up(a, t):
        n = a * 4 + t
        dst = ubuf.at[n]
        if t == 0:
            src = yz.at[a, (y + UPS[a]) % NY]
        else:
            src = ubuf.at[n - 1]
            rcopy(src, src, us.at[n - 1], ur.at[n - 1], up).wait_recv()
            ubuf[n - 1] = ubuf[n - 1] + yz[a, (y + UPS[a] - t) % NY]
        send(src, dst, us.at[n], ur.at[n], up)

    def sum_down(a, t):
        n = a * 4 + t
        dst = dbuf.at[n]
        if t == 0:
            src = yz.at[a, (y + NY - DOWNS[a]) % NY]
        else:
            src = dbuf.at[n - 1]
            rcopy(src, src, ds.at[n - 1], dr.at[n - 1], down).wait_recv()
            dbuf[n - 1] = dbuf[n - 1] + yz[a, (y + NY - DOWNS[a] + t) % NY]
        send(src, dst, ds.at[n], dr.at[n], down)

    def sum_step(t):
        for a in range(2):
            if t < UPS[a]:
                sum_up(a, t)
            if t < DOWNS[a]:
                sum_down(a, t)

    sum_step(0)

    def put(m, mat):
        for n in range(2):
            aue[n, m] = mat[:, n * 128 : (n + 1) * 128]
        send(aue.at[1 - k, m], kbuf.at[m], ks.at[m], kr.at[m], core)

    pp = halves(c_ref[:, :, W : W + ROWS].reshape(W, ROWS))
    qp = halves(c_ref[:, :, W + ROWS : OWN].reshape(W, ROWS))
    ysp = halves(yv[...])
    a_mat = dot3(pp, ysp, NN)
    put(0, a_mat)
    uv[...] = dot3(halves(a_mat), top, NN) - dot3(qp, ysp, NN).T
    first = jnp.where(p == 0, 1.0, 0.0)
    mid = pl.ds(pl.multiple_of(q * SHARE, SHARE), SHARE)
    uv[mid, :] = uv[mid, :] - first * dot3(halves(d_ref[...]), top, NN)
    u_mat = uv[...]
    put(1, u_mat)
    sum_step(1)
    e_mat = -dot3(halves(topf.T), halves(u_mat), NN) - dot3(qp, halves(zv[...]), NN)
    put(2, e_mat)
    sum_step(2)

    busy = x < 3

    def xcopy(m, d):
        return rcopy(acc.at[m], xbuf.at[d - 1], xs.at[d - 1], xr.at[d - 1], xk[d, 0])

    for m in range(3):
        got = kbuf.at[m]
        rcopy(got, got, ks.at[m], kr.at[m], core).wait_recv()
        acc[m] = aue[k, m] + kbuf[m]
    for d in (2, 1, 3):
        m = (x + d) % NX

        @pl.when(m < 3)
        def _():
            xcopy(m, d).start()

    sum_step(3)

    for a in range(2):
        n = a * 4 + UPS[a] - 1
        got = ubuf.at[n]
        rcopy(got, got, us.at[n], ur.at[n], up).wait_recv()
        n2 = a * 4 + DOWNS[a] - 1
        got = dbuf.at[n2]
        rcopy(got, got, ds.at[n2], dr.at[n2], down).wait_recv()
        yzacc[a] = yz[a, y] + (ubuf[n] + dbuf[n2])
    send(yzacc.at[1 - zh], hbuf, hs.at[0], hr.at[0], far)

    def ycopy(d):
        return rcopy(accx.at[:, (y + d) % NY], ybuf.at[d - 1], ys.at[d - 1], yr.at[d - 1], ydev[d])

    def zcopy(d):
        return rcopy(accy.at[zpos[d] // NZL], zbuf.at[d - 1], zs.at[d - 1], zr.at[d - 1], zdev[d])

    def fcopy(d, f):
        n = d * 2 + f - 1
        return rcopy(auo.at[x, k], auo.at[x, k], fs.at[n], fr.at[n], xk[d, f])

    @pl.when(busy)
    def _():
        for d in range(1, NX):
            xcopy(x, d).wait_recv()
        total = (acc[x] + xbuf[0]) + (xbuf[1] + xbuf[2])
        accx[...] = total.reshape(NZH, NY, SHARE, 128)
        for d in (4, 3, 5, 2, 6, 1, 7):
            ycopy(d).start()

    hop = rcopy(hbuf, hbuf, hs.at[0], hr.at[0], far)
    hop.wait_recv()
    yzo[...] = yzacc[zh] + hbuf[...]

    @pl.when(busy)
    def _():
        for d in range(1, NY):
            ycopy(d).wait_recv()
        total = accx[:, y]
        for d in range(NY - 1):
            total = total + ybuf[d]
        accy[...] = total
        for d in (4, 3, 5, 2, 6, 1, 7):
            zcopy(d).start()
        for d in range(1, NZ):
            zcopy(d).wait_recv()
        total = accy[zh]
        for d in range(NZ - 1):
            total = total + zbuf[d]
        auo[x, k] = total
        for d, f in xk:
            fcopy(d, f).start()

    for d, f in xk:
        m = (x + NX - d) % NX
        n = d * 2 + f - 1

        @pl.when(m < 3)
        def _():
            got = auo.at[m, k if f == 0 else 1 - k]
            rcopy(got, got, fs.at[n], fr.at[n], xk[d, f]).wait_recv()

    @pl.when(jnp.logical_not(fixed))
    def _():
        out.wait_send()

    for copy in sends:
        copy.wait_send()
    for d in (2, 1, 3):
        m = (x + d) % NX

        @pl.when(m < 3)
        def _():
            xcopy(m, d).wait_send()

    @pl.when(busy)
    def _():
        for d in range(1, NY):
            ycopy(d).wait_send()
        for d in range(1, NZ):
            zcopy(d).wait_send()
        for d, f in xk:
            fcopy(d, f).wait_send()


def step(*operands):
    vmem = pl.BlockSpec(memory_space=pltpu.VMEM)
    smem = pl.BlockSpec(memory_space=pltpu.SMEM)
    dma = pltpu.SemaphoreType.DMA
    rows = SL * CB
    buffers = [
        (RC * B * 8, B),
        (ROWS, 8 * B),
        (ROWS, 2 * ROWS),
        (SHARE, WIDE),
        (NROW, SHARE, PATCH),
        (NCOL, SHARE, OWN),
        (ROWS, W),
        (ROWS, W),
        (W, W),
        (NZH, NY, rows, 2 * W),
        (2, 3, W, 128),
        (3, W, 128),
        (3, W, 128),
        (3, W, 128),
        (NZH, NY, SHARE, 128),
        (NY - 1, NZH, SHARE, 128),
        (NZH, SHARE, 128),
        (NZ - 1, SHARE, 128),
        (8, rows, 2 * W),
        (8, rows, 2 * W),
        (NZH, rows, 2 * W),
        (rows, 2 * W),
    ]
    sems = [1, 1, 1, 1, 3, 3, 12, 12, 16, 16, 1, 1, 8, 8, 8, 8]
    sems += [3, 3, 3, 3, 7, 7, 7, 7, 7, 7, 8, 8, 8, 8, 1, 1]
    return pl.pallas_call(
        step_kernel,
        out_shape=(
            jax.ShapeDtypeStruct((rows, 2 * W), F32),
            jax.ShapeDtypeStruct((3, 2, SHARE, 128), F32),
        ),
        in_specs=[smem] * 3 + [pl.BlockSpec(memory_space=pl.ANY)] + [vmem] * 4,
        out_specs=(vmem, vmem),
        scratch_shapes=[pltpu.VMEM(b, F32) for b in buffers] + [dma((n,)) for n in sems],
        compiler_params=pltpu.CompilerParams(collective_id=0, has_side_effects=True),
        name="step",
    )(*operands)


def place_kernel(pb, yz_ref, mats_ref, d_ref, cd_ref, prow, pd, crow, cu, cdiag):
    p = lax.axis_index("row")
    for r in range(RC):
        ya = jnp.zeros((CB, W), F32)
        za = jnp.zeros((CB, W), F32)
        for s in range(SL):
            here = pb[s] == r * NROW + p
            ya = jnp.where(here, yz_ref[s * CB : (s + 1) * CB, 0:W], ya)
            za = jnp.where(here, yz_ref[s * CB : (s + 1) * CB, W:], za)
        prow[r] = ya
        crow[r] = za
    for n in range(2):
        at = slice(n * 128, (n + 1) * 128)
        pd[:, at] = d_ref[:, at] - mats_ref[0, n]
        cu[:, at] = mats_ref[1, n]
        cdiag[:, at] = cd_ref[:, at] + mats_ref[2, n]


def lay(*operands):
    vmem = pl.BlockSpec(memory_space=pltpu.VMEM)
    smem = pl.BlockSpec(memory_space=pltpu.SMEM)
    share = jax.ShapeDtypeStruct((SHARE, W), F32)
    rows = jax.ShapeDtypeStruct((RC, CB, W), F32)
    return pl.pallas_call(
        place_kernel,
        out_shape=(rows, share, rows, share, share),
        in_specs=[smem] + [vmem] * 4,
        out_specs=(vmem,) * 5,
        name="lay",
    )(*operands)


def body(
    cached_inverse,
    parent_panel,
    parent_blocks,
    parent_sizes,
    parent_diagonal,
    child_panel,
    child_top,
    child_blocks,
    child_sizes,
    child_diagonal,
):
    rows, mats = step(
        parent_blocks,
        parent_sizes,
        child_sizes,
        cached_inverse.reshape(RC * B * 8, B),
        jnp.transpose(parent_panel, (1, 0, 2)),
        jnp.transpose(child_panel, (1, 0, 2)),
        child_top,
        parent_diagonal,
    )
    prow, pd, crow, cu, cdiag = lay(parent_blocks, rows, mats, parent_diagonal, child_diagonal)
    return (prow[:, None], pd, crow[:, None], cu, cdiag)


def solution(mesh):
    in_specs = (
        P(None, "row", None, None, "col", None),
        P("col", "row", None),
        P("row"),
        P("row"),
        P("col", None),
        P("col", "row", None),
        P("col", None),
        P("row"),
        P("row"),
        P("col", None),
    )
    out_specs = (
        P(None, "row", "col", None),
        P("col", None),
        P(None, "row", "col", None),
        P("col", None),
        P("col", None),
    )
    return jax.shard_map(body, mesh=mesh, in_specs=in_specs, out_specs=out_specs, check_vma=False)
```

```python
import jax
import jax.numpy as jnp
from jax import lax
from jax.experimental import pallas as pl
from jax.experimental.pallas import tpu as pltpu
from jax.sharding import PartitionSpec as P

MESH = pl.DeviceIdType.MESH
F32 = jnp.float32
BF16 = jnp.bfloat16

NX, NZL, NZH, NY, NK = 4, 4, 2, 8, 2
NZ = NZL * NZH
NROW, NCOL = NX * NZL * NK, NZH * NY
W, B, SL, RC = 256, 128, 3, 4
SHARE = W // NCOL
ROWS = SL * B
CB = B // NCOL
PATCH = 2 * ROWS + 128
OWN = W + 2 * ROWS
WIDE = W + PATCH
UPS = (4, 3)
DOWNS = (3, 4)


def place():
    p = lax.axis_index("row")
    q = lax.axis_index("col")
    x = p // (NZL * NK)
    zl = (p // NK) % NZL
    k = p % NK
    return p, q, x, zl, k, q // NY, q % NY


def row_id(x, zl, k):
    return (x * NZL + zl) * NK + k


def rcopy(src, dst, send, recv, target):
    return pltpu.make_async_remote_copy(
        src_ref=src,
        dst_ref=dst,
        send_sem=send,
        recv_sem=recv,
        device_id=target,
        device_id_type=MESH,
    )


def halves(a):
    hi = a.astype(BF16)
    lo = (a - hi.astype(F32)).astype(BF16)
    return hi, lo


def dot3(a, b, dims):
    def one(u, v):
        return lax.dot_general(u, v, (dims, ((), ())), preferred_element_type=F32)

    return one(a[0], b[0]) + (one(a[0], b[1]) + one(a[1], b[0]))


NN = ((1,), (0,))
NT = ((1,), (1,))


def pick(values, which, first=0):
    out = values[0]
    for n in range(1, len(values)):
        out = jnp.where(which == n, values[n], out)
    return out


def step_kernel(
    pb, psz, csz, s_hbm, pp_ref, cp_ref, top_ref, d_ref,
    yzo, auo,
    sv, sub8, sub, xv, g_ref, c_ref, yv, zv, uv, yz, aue,
    kbuf, acc, xbuf, accx, ybuf, accy, zbuf, ubuf, dbuf, yzacc, hbuf,
    ssem, ps, pr, lsem, gzs, gzr, gxs, gxr, gks, gkr, chs, chr_, cus, cur, cds, cdr,
    ks, kr, xs, xr, ys, yr, zs, zr, fs, fr, us, ur, ds, dr, hs, hr,
):
    p, q, x, zl, k, zh, y = place()
    z = zh * NZL + zl
    half, cls = p // NCOL, p % NCOL
    fixed = q == cls
    swap = (half * NCOL + q, cls)
    xk = {}
    for d in range(NX):
        for f in range(2):
            if d or f:
                xk[d, f] = (row_id((x + d) % NX, zl, k if f == 0 else 1 - k), q)
    core = xk[0, 1]
    lzdev = [None] + [(row_id(x, (zl + d) % NZL, k), q) for d in range(1, NZL)]
    ydev = [None] + [(p, zh * NY + (y + d) % NY) for d in range(1, NY)]
    up, down = ydev[1], ydev[NY - 1]
    zpos = [(z + d) % NZ for d in range(NZ)]
    zdev = [None] + [(row_id(x, zpos[d] % NZL, k), (zpos[d] // NZL) * NY + y) for d in range(1, NZ)]
    far = zdev[NZL]

    load_s = pltpu.make_async_copy(s_hbm, sv, ssem.at[0])
    load_s.start()

    barrier = pltpu.get_barrier_semaphore()

    @pl.when(jnp.logical_not(fixed))
    def _():
        pl.semaphore_signal(barrier, inc=1, device_id=swap, device_id_type=MESH)

    for dev in zdev[1:] + ydev[1:] + list(xk.values()):
        pl.semaphore_signal(barrier, inc=1, device_id=dev, device_id_type=MESH)

    lane = lax.broadcasted_iota(jnp.int32, (SHARE, B), 1)
    xv[:, 0:W] = top_ref[...]
    for s in range(SL):
        at = W + s * B
        xv[:, at : at + B] = jnp.where(lane < psz[s], pp_ref[s], 0.0)
        at += ROWS
        xv[:, at : at + B] = jnp.where(lane < csz[s], cp_ref[s], 0.0)
    local = [jnp.maximum(pb[s], 0) // NROW for s in range(SL)]
    tag = jnp.zeros((SHARE, 128), F32)
    tags = lax.broadcasted_iota(jnp.int32, (SHARE, 128), 1)
    for s in range(SL):
        tag = jnp.where(tags == s, local[s].astype(F32), tag)
    xv[:, OWN:WIDE] = tag
    c_ref[q] = xv[:, 0:OWN]

    pl.semaphore_wait(barrier, 7 + NY - 1 + NZ - 1 + jnp.where(fixed, 0, 1))

    sends = []

    def send(*args):
        copy = rcopy(*args)
        copy.start()
        sends.append(copy)

    piece = xv.at[:, W:WIDE]
    mine = xv.at[:, 0:OWN]
    out = rcopy(piece, g_ref.at[half * NCOL + q], ps.at[0], pr.at[0], swap)
    keep = pltpu.make_async_copy(piece, g_ref.at[p], lsem.at[0])

    @pl.when(jnp.logical_not(fixed))
    def _():
        out.start()

    @pl.when(fixed)
    def _():
        keep.start()

    def ring(a, t, src_up, src_down):
        zz = zh if a == 0 else 1 - zh
        if src_up is not None:
            at = zz * NY + (y + NY - t) % NY
            send(src_up, c_ref.at[at], cus.at[a * 4 + t], cur.at[a * 4 + t], up)
        if src_down is not None:
            at = zz * NY + (y + t) % NY
            send(src_down, c_ref.at[at], cds.at[a * 4 + t], cdr.at[a * 4 + t], down)

    def ring_up_wait(a, t):
        zz = zh if a == 0 else 1 - zh
        got = c_ref.at[zz * NY + (y + NY - 1 - t) % NY]
        rcopy(got, got, cus.at[a * 4 + t], cur.at[a * 4 + t], up).wait_recv()
        if t + 1 < UPS[a]:
            ring(a, t + 1, got, None)

    def ring_down_wait(a, t):
        zz = zh if a == 0 else 1 - zh
        got = c_ref.at[zz * NY + (y + 1 + t) % NY]
        rcopy(got, got, cds.at[a * 4 + t], cdr.at[a * 4 + t], down).wait_recv()
        if t + 1 < DOWNS[a]:
            ring(a, t + 1, None, got)

    send(mine, c_ref.at[q], chs.at[0], chr_.at[0], far)
    ring(0, 0, mine, mine)

    load_s.wait()
    for s in range(SL):
        for c in range(8):
            blocks = [sv[pl.ds(r * B * 8 + c, B, stride=8), :] for r in range(RC)]
            sub8[s * B : (s + 1) * B, c * B : (c + 1) * B] = pick(blocks, local[s])

    def ring_wait(a, t):
        if t < UPS[a]:
            ring_up_wait(a, t)
        if t < DOWNS[a]:
            ring_down_wait(a, t)

    ring_wait(0, 0)
    ring_wait(0, 1)
    other = c_ref.at[(1 - zh) * NY + y]
    rcopy(other, other, chs.at[0], chr_.at[0], far).wait_recv()
    ring(1, 0, other, other)

    @pl.when(jnp.logical_not(fixed))
    def _():
        rcopy(piece, g_ref.at[p], ps.at[0], pr.at[0], swap).wait_recv()

    @pl.when(fixed)
    def _():
        keep.wait()

    def fan(src, dz):
        got = g_ref.at[src]
        for d in (1, 3) if dz == 0 else (2, 1, 3):
            send(got, got, gxs.at[dz * 3 + d - 1], gxr.at[dz * 3 + d - 1], xk[d, 0])
        send(got, got, gks.at[dz * 4], gkr.at[dz * 4], core)

    own = g_ref.at[p]
    for d in (1, 3, 2):
        send(own, own, gzs.at[d - 1], gzr.at[d - 1], lzdev[d])
    fan(p, 0)

    def z_wait(d):
        src = row_id(x, (zl + NZL - d) % NZL, k)
        got = g_ref.at[src]
        rcopy(got, got, gzs.at[d - 1], gzr.at[d - 1], lzdev[d]).wait_recv()
        fan(src, d)

    def x_wait(dz, d):
        src = row_id((x + NX - d) % NX, (zl + NZL - dz) % NZL, k)
        got = g_ref.at[src]
        n = dz * 3 + d - 1
        rcopy(got, got, gxs.at[n], gxr.at[n], xk[d, 0]).wait_recv()
        n = dz * 3 + 1
        if dz == 0 and d == 1:
            send(got, got, gxs.at[n], gxr.at[n], xk[d, 0])
        send(got, got, gks.at[dz * 4 + d], gkr.at[dz * 4 + d], core)

    ring_wait(0, 2)
    ring_wait(1, 0)
    z_wait(1)
    z_wait(3)
    x_wait(0, 1)
    x_wait(0, 3)
    ring_wait(1, 1)
    z_wait(2)
    x_wait(0, 2)
    ring_wait(0, 3)
    x_wait(1, 1)
    x_wait(1, 3)
    x_wait(3, 1)
    x_wait(3, 3)

    def heard(slot):
        tile = g_ref[slot, 0:8, 2 * ROWS : 2 * ROWS + 128]
        return [jnp.max(jnp.where(tags[0:8] == t, tile, 0.0)) for t in range(SL)]

    ours, theirs = heard(p), heard(row_id((x + 2) % NX, zl, k))
    for h in range(2):
        for t in range(SL):
            which = jnp.where(half == h, ours[t], theirs[t])
            for s in range(SL):
                at = slice(s * B, (s + 1) * B)
                n = h * SL + t
                value = sub8[at, h * B : (h + 1) * B]
                for r in range(1, RC):
                    block = sub8[at, (2 * r + h) * B : (2 * r + h + 1) * B]
                    value = jnp.where(which > r - 0.5, block, value)
                sub[at, n * B : (n + 1) * B] = value

    x_wait(1, 2)
    x_wait(3, 2)
    x_wait(2, 1)
    x_wait(2, 3)
    x_wait(2, 2)
    ring_wait(1, 2)
    for dz in (0, 1, 3, 2):
        for d in (0, 1, 3, 2):
            src = row_id((x + NX - d) % NX, (zl + NZL - dz) % NZL, 1 - k)
            got = g_ref.at[src]
            rcopy(got, got, gks.at[dz * 4 + d], gkr.at[dz * 4 + d], core).wait_recv()

    def panel(h, at):
        return halves(g_ref[h * NCOL : (h + 1) * NCOL, :, at : at + ROWS].reshape(W, ROWS))

    gp = [panel(h, 0) for h in range(2)]
    gq = [panel(h, ROWS) for h in range(2)]
    for s in range(SL):
        at = slice(s * B, (s + 1) * B)
        left = [halves(sub[at, h * ROWS : (h + 1) * ROWS]) for h in range(2)]
        yv[at, :] = dot3(left[0], gp[0], NT) + dot3(left[1], gp[1], NT)
        zv[at, :] = dot3(left[0], gq[0], NT) + dot3(left[1], gq[1], NT)
    ring_wait(1, 3)
    topf = c_ref[:, :, 0:W].reshape(W, W)
    top = halves(topf)
    rows = lax.broadcasted_iota(jnp.int32, (B, 1), 0)
    for s in range(SL):
        at = slice(s * B, (s + 1) * B)
        yy = jnp.where(rows < psz[s], -yv[at, :], 0.0)
        zz = jnp.where(rows < csz[s], -(zv[at, :] + dot3(halves(yy), top, NN)), 0.0)
        yv[at, :] = yy
        zv[at, :] = zz
        yz[:, :, s * CB : (s + 1) * CB, 0:W] = yy.reshape(NZH, NY, CB, W)
        yz[:, :, s * CB : (s + 1) * CB, W : 2 * W] = zz.reshape(NZH, NY, CB, W)

    def sum_up(a, t):
        n = a * 4 + t
        dst = ubuf.at[n]
        if t == 0:
            src = yz.at[a, (y + UPS[a]) % NY]
        else:
            src = ubuf.at[n - 1]
            rcopy(src, src, us.at[n - 1], ur.at[n - 1], up).wait_recv()
            ubuf[n - 1] = ubuf[n - 1] + yz[a, (y + UPS[a] - t) % NY]
        send(src, dst, us.at[n], ur.at[n], up)

    def sum_down(a, t):
        n = a * 4 + t
        dst = dbuf.at[n]
        if t == 0:
            src = yz.at[a, (y + NY - DOWNS[a]) % NY]
        else:
            src = dbuf.at[n - 1]
            rcopy(src, src, ds.at[n - 1], dr.at[n - 1], down).wait_recv()
            dbuf[n - 1] = dbuf[n - 1] + yz[a, (y + NY - DOWNS[a] + t) % NY]
        send(src, dst, ds.at[n], dr.at[n], down)

    def sum_step(t):
        for a in range(2):
            if t < UPS[a]:
                sum_up(a, t)
            if t < DOWNS[a]:
                sum_down(a, t)

    sum_step(0)

    def put(m, mat):
        for n in range(2):
            aue[n, m] = mat[:, n * 128 : (n + 1) * 128]
        send(aue.at[1 - k, m], kbuf.at[m], ks.at[m], kr.at[m], core)

    pp = halves(c_ref[:, :, W : W + ROWS].reshape(W, ROWS))
    qp = halves(c_ref[:, :, W + ROWS : OWN].reshape(W, ROWS))
    ysp = halves(yv[...])
    a_mat = dot3(pp, ysp, NN)
    put(0, a_mat)
    uv[...] = dot3(halves(a_mat), top, NN) - dot3(qp, ysp, NN).T
    first = jnp.where(p == 0, 1.0, 0.0)
    mid = pl.ds(pl.multiple_of(q * SHARE, SHARE), SHARE)
    uv[mid, :] = uv[mid, :] - first * dot3(halves(d_ref[...]), top, NN)
    u_mat = uv[...]
    put(1, u_mat)
    sum_step(1)
    e_mat = -dot3(halves(topf.T), halves(u_mat), NN) - dot3(qp, halves(zv[...]), NN)
    put(2, e_mat)

    busy = x < 3
    ahead, behind = xk[1, 0], xk[3, 0]
    nxt, prv = (x + 1) % NX, (x + 3) % NX

    def xcopy(n, m, part, dev):
        return rcopy(acc.at[m, part], xbuf.at[n], xs.at[n], xr.at[n], dev)

    def landed(n, dev):
        rcopy(xbuf.at[n], xbuf.at[n], xs.at[n], xr.at[n], dev).wait_recv()

    def relay_up():
        return xcopy(0, (x + 2) % NX, 1, ahead)

    def relay_down():
        return xcopy(1, (x + 2) % NX, 0, behind)

    def plain_up():
        return xcopy(2, nxt, 0, ahead)

    def plain_down():
        return xcopy(3, prv, 1, behind)

    def total_up():
        return xcopy(4, nxt, 1, ahead)

    def total_down():
        return xcopy(5, prv, 0, behind)

    for m in range(3):
        got = kbuf.at[m]
        rcopy(got, got, ks.at[m], kr.at[m], core).wait_recv()
        acc[m] = (aue[k, m] + kbuf[m]).reshape(2, 128, 128)
        rel = (m + NX - x) % NX

        @pl.when(rel == 2)
        def _():
            relay_up().start()
            relay_down().start()

        @pl.when(rel == 1)
        def _():
            plain_up().start()

        @pl.when(rel == 3)
        def _():
            plain_down().start()

    sum_step(2)

    @pl.when(nxt < 3)
    def _():
        landed(0, ahead)
        acc[nxt, 1] = acc[nxt, 1] + xbuf[0]
        total_up().start()

    @pl.when(prv < 3)
    def _():
        landed(1, behind)
        acc[prv, 0] = acc[prv, 0] + xbuf[1]
        total_down().start()

    sum_step(3)

    def ycopy(d):
        return rcopy(accx.at[:, (y + d) % NY], ybuf.at[d - 1], ys.at[d - 1], yr.at[d - 1], ydev[d])

    def zcopy(d):
        return rcopy(accy.at[zpos[d] // NZL], zbuf.at[d - 1], zs.at[d - 1], zr.at[d - 1], zdev[d])

    def fcopy(d, f):
        n = d * 2 + f - 1
        return rcopy(auo.at[x, k], auo.at[x, k], fs.at[n], fr.at[n], xk[d, f])

    @pl.when(busy)
    def _():
        for n in range(2, 6):
            landed(n, ahead if n % 2 == 0 else behind)
        low = acc[x, 0] + (xbuf[2] + xbuf[5])
        high = acc[x, 1] + (xbuf[3] + xbuf[4])
        accx[0] = low.reshape(NY, SHARE, 128)
        accx[1] = high.reshape(NY, SHARE, 128)
        for d in (4, 3, 5, 2, 6, 1, 7):
            ycopy(d).start()

    for a in range(2):
        n = a * 4 + UPS[a] - 1
        got = ubuf.at[n]
        rcopy(got, got, us.at[n], ur.at[n], up).wait_recv()
        n2 = a * 4 + DOWNS[a] - 1
        got = dbuf.at[n2]
        rcopy(got, got, ds.at[n2], dr.at[n2], down).wait_recv()
        yzacc[a] = yz[a, y] + (ubuf[n] + dbuf[n2])
    send(yzacc.at[1 - zh], hbuf, hs.at[0], hr.at[0], far)

    hop = rcopy(hbuf, hbuf, hs.at[0], hr.at[0], far)
    @pl.when(busy)
    def _():
        for d in range(1, NY):
            ycopy(d).wait_recv()
        total = accx[:, y]
        for d in range(NY - 1):
            total = total + ybuf[d]
        accy[...] = total
        for d in (4, 3, 5, 2, 6, 1, 7):
            zcopy(d).start()

    hop.wait_recv()
    yzo[...] = yzacc[zh] + hbuf[...]

    @pl.when(busy)
    def _():
        for d in range(1, NZ):
            zcopy(d).wait_recv()
        total = accy[zh]
        for d in range(NZ - 1):
            total = total + zbuf[d]
        auo[x, k] = total
        for d, f in xk:
            fcopy(d, f).start()

    for d, f in xk:
        m = (x + NX - d) % NX
        n = d * 2 + f - 1

        @pl.when(m < 3)
        def _():
            got = auo.at[m, k if f == 0 else 1 - k]
            rcopy(got, got, fs.at[n], fr.at[n], xk[d, f]).wait_recv()

    @pl.when(jnp.logical_not(fixed))
    def _():
        out.wait_send()

    for copy in sends:
        copy.wait_send()

    @pl.when((x + 2) % NX < 3)
    def _():
        relay_up().wait_send()
        relay_down().wait_send()

    @pl.when(nxt < 3)
    def _():
        plain_up().wait_send()
        total_up().wait_send()

    @pl.when(prv < 3)
    def _():
        plain_down().wait_send()
        total_down().wait_send()

    @pl.when(busy)
    def _():
        for d in range(1, NY):
            ycopy(d).wait_send()
        for d in range(1, NZ):
            zcopy(d).wait_send()
        for d, f in xk:
            fcopy(d, f).wait_send()


def step(*operands):
    vmem = pl.BlockSpec(memory_space=pltpu.VMEM)
    smem = pl.BlockSpec(memory_space=pltpu.SMEM)
    dma = pltpu.SemaphoreType.DMA
    rows = SL * CB
    buffers = [
        (RC * B * 8, B),
        (ROWS, 8 * B),
        (ROWS, 2 * ROWS),
        (SHARE, WIDE),
        (NROW, SHARE, PATCH),
        (NCOL, SHARE, OWN),
        (ROWS, W),
        (ROWS, W),
        (W, W),
        (NZH, NY, rows, 2 * W),
        (2, 3, W, 128),
        (3, W, 128),
        (3, 2, 128, 128),
        (6, 128, 128),
        (NZH, NY, SHARE, 128),
        (NY - 1, NZH, SHARE, 128),
        (NZH, SHARE, 128),
        (NZ - 1, SHARE, 128),
        (8, rows, 2 * W),
        (8, rows, 2 * W),
        (NZH, rows, 2 * W),
        (rows, 2 * W),
    ]
    sems = [1, 1, 1, 1, 3, 3, 12, 12, 16, 16, 1, 1, 8, 8, 8, 8]
    sems += [3, 3, 6, 6, 7, 7, 7, 7, 7, 7, 8, 8, 8, 8, 1, 1]
    return pl.pallas_call(
        step_kernel,
        out_shape=(
            jax.ShapeDtypeStruct((rows, 2 * W), F32),
            jax.ShapeDtypeStruct((3, 2, SHARE, 128), F32),
        ),
        in_specs=[smem] * 3 + [pl.BlockSpec(memory_space=pl.ANY)] + [vmem] * 4,
        out_specs=(vmem, vmem),
        scratch_shapes=[pltpu.VMEM(b, F32) for b in buffers] + [dma((n,)) for n in sems],
        compiler_params=pltpu.CompilerParams(collective_id=0, has_side_effects=True),
        name="step",
    )(*operands)


def place_kernel(pb, yz_ref, mats_ref, d_ref, cd_ref, prow, pd, crow, cu, cdiag):
    p = lax.axis_index("row")
    for r in range(RC):
        ya = jnp.zeros((CB, W), F32)
        za = jnp.zeros((CB, W), F32)
        for s in range(SL):
            here = pb[s] == r * NROW + p
            ya = jnp.where(here, yz_ref[s * CB : (s + 1) * CB, 0:W], ya)
            za = jnp.where(here, yz_ref[s * CB : (s + 1) * CB, W:], za)
        prow[r] = ya
        crow[r] = za
    for n in range(2):
        at = slice(n * 128, (n + 1) * 128)
        pd[:, at] = d_ref[:, at] - mats_ref[0, n]
        cu[:, at] = mats_ref[1, n]
        cdiag[:, at] = cd_ref[:, at] + mats_ref[2, n]


def lay(*operands):
    vmem = pl.BlockSpec(memory_space=pltpu.VMEM)
    smem = pl.BlockSpec(memory_space=pltpu.SMEM)
    share = jax.ShapeDtypeStruct((SHARE, W), F32)
    rows = jax.ShapeDtypeStruct((RC, CB, W), F32)
    return pl.pallas_call(
        place_kernel,
        out_shape=(rows, share, rows, share, share),
        in_specs=[smem] + [vmem] * 4,
        out_specs=(vmem,) * 5,
        name="lay",
    )(*operands)


def body(
    cached_inverse,
    parent_panel,
    parent_blocks,
    parent_sizes,
    parent_diagonal,
    child_panel,
    child_top,
    child_blocks,
    child_sizes,
    child_diagonal,
):
    rows, mats = step(
        parent_blocks,
        parent_sizes,
        child_sizes,
        cached_inverse.reshape(RC * B * 8, B),
        jnp.transpose(parent_panel, (1, 0, 2)),
        jnp.transpose(child_panel, (1, 0, 2)),
        child_top,
        parent_diagonal,
    )
    prow, pd, crow, cu, cdiag = lay(parent_blocks, rows, mats, parent_diagonal, child_diagonal)
    return (prow[:, None], pd, crow[:, None], cu, cdiag)


def solution(mesh):
    in_specs = (
        P(None, "row", None, None, "col", None),
        P("col", "row", None),
        P("row"),
        P("row"),
        P("col", None),
        P("col", "row", None),
        P("col", None),
        P("row"),
        P("row"),
        P("col", None),
    )
    out_specs = (
        P(None, "row", "col", None),
        P("col", None),
        P(None, "row", "col", None),
        P("col", None),
        P("col", None),
    )
    return jax.shard_map(body, mesh=mesh, in_specs=in_specs, out_specs=out_specs, check_vma=False)
```

```python
import jax
import jax.numpy as jnp
from jax import lax
from jax.experimental import pallas as pl
from jax.experimental.pallas import tpu as pltpu
from jax.sharding import PartitionSpec as P

MESH = pl.DeviceIdType.MESH
F32 = jnp.float32
BF16 = jnp.bfloat16

NX, NZL, NZH, NY, NK = 4, 4, 2, 8, 2
NZ = NZL * NZH
NROW, NCOL = NX * NZL * NK, NZH * NY
W, B, SL, RC = 256, 128, 3, 4
SHARE = W // NCOL
ROWS = SL * B
CB = B // NCOL
PATCH = 2 * ROWS + 128
OWN = W + 2 * ROWS
WIDE = W + PATCH
UPS = (4, 3)
DOWNS = (3, 4)


def place():
    p = lax.axis_index("row")
    q = lax.axis_index("col")
    x = p // (NZL * NK)
    zl = (p // NK) % NZL
    k = p % NK
    return p, q, x, zl, k, q // NY, q % NY


def row_id(x, zl, k):
    return (x * NZL + zl) * NK + k


def rcopy(src, dst, send, recv, target):
    return pltpu.make_async_remote_copy(
        src_ref=src,
        dst_ref=dst,
        send_sem=send,
        recv_sem=recv,
        device_id=target,
        device_id_type=MESH,
    )


def halves(a):
    hi = a.astype(BF16)
    lo = (a - hi.astype(F32)).astype(BF16)
    return hi, lo


def dot3(a, b, dims):
    def one(u, v):
        return lax.dot_general(u, v, (dims, ((), ())), preferred_element_type=F32)

    return one(a[0], b[0]) + (one(a[0], b[1]) + one(a[1], b[0]))


NN = ((1,), (0,))
NT = ((1,), (1,))


def pick(values, which, first=0):
    out = values[0]
    for n in range(1, len(values)):
        out = jnp.where(which == n, values[n], out)
    return out


def step_kernel(
    pb_hbm, psz_hbm, csz_hbm, s_hbm, pp_hbm, cp_hbm, top_hbm, d_hbm,
    yzo, auo,
    pb, psz, csz, pp_ref, cp_ref, d_ref, sv, sub8, sub, xv, g_ref, c_ref, yv, zv, uv, yz, aue,
    kbuf, acc, xbuf, accx, ybuf, accy, zbuf, ubuf, dbuf, yzacc, hbuf,
    ssem, isem, ps, pr, lsem, gzs, gzr, gxs, gxr, gks, gkr, chs, chr_, cus, cur, cds, cdr,
    ks, kr, xs, xr, ys, yr, zs, zr, fs, fr, us, ur, ds, dr, hs, hr,
):
    p, q, x, zl, k, zh, y = place()
    z = zh * NZL + zl
    half, cls = p // NCOL, p % NCOL
    fixed = q == cls
    swap = (half * NCOL + q, cls)
    xk = {}
    for d in range(NX):
        for f in range(2):
            if d or f:
                xk[d, f] = (row_id((x + d) % NX, zl, k if f == 0 else 1 - k), q)
    core = xk[0, 1]
    lzdev = [None] + [(row_id(x, (zl + d) % NZL, k), q) for d in range(1, NZL)]
    ydev = [None] + [(p, zh * NY + (y + d) % NY) for d in range(1, NY)]
    up, down = ydev[1], ydev[NY - 1]
    zpos = [(z + d) % NZ for d in range(NZ)]
    zdev = [None] + [(row_id(x, zpos[d] % NZL, k), (zpos[d] // NZL) * NY + y) for d in range(1, NZ)]
    far = zdev[NZL]

    barrier = pltpu.get_barrier_semaphore()

    @pl.when(jnp.logical_not(fixed))
    def _():
        pl.semaphore_signal(barrier, inc=1, device_id=swap, device_id_type=MESH)

    for dev in zdev[1:] + ydev[1:] + list(xk.values()):
        pl.semaphore_signal(barrier, inc=1, device_id=dev, device_id_type=MESH)

    loads = [
        pltpu.make_async_copy(src, dst, isem.at[n])
        for n, (src, dst) in enumerate((
            (psz_hbm, psz),
            (csz_hbm, csz),
            (pb_hbm, pb),
            (pp_hbm, pp_ref),
            (cp_hbm, cp_ref),
            (top_hbm, xv.at[:, 0:W]),
            (d_hbm, d_ref),
        ))
    ]
    for load in loads:
        load.start()
    load_s = pltpu.make_async_copy(s_hbm, sv, ssem.at[0])
    load_s.start()
    for load in loads:
        load.wait()

    lane = lax.broadcasted_iota(jnp.int32, (SHARE, B), 1)
    for s in range(SL):
        at = W + s * B
        xv[:, at : at + B] = jnp.where(lane < psz[s], pp_ref[s], 0.0)
        at += ROWS
        xv[:, at : at + B] = jnp.where(lane < csz[s], cp_ref[s], 0.0)
    local = [jnp.maximum(pb[s], 0) // NROW for s in range(SL)]
    tag = jnp.zeros((SHARE, 128), F32)
    tags = lax.broadcasted_iota(jnp.int32, (SHARE, 128), 1)
    for s in range(SL):
        tag = jnp.where(tags == s, local[s].astype(F32), tag)
    xv[:, OWN:WIDE] = tag
    c_ref[q] = xv[:, 0:OWN]

    pl.semaphore_wait(barrier, 7 + NY - 1 + NZ - 1 + jnp.where(fixed, 0, 1))

    sends = []

    def send(*args):
        copy = rcopy(*args)
        copy.start()
        sends.append(copy)

    piece = xv.at[:, W:WIDE]
    mine = xv.at[:, 0:OWN]
    out = rcopy(piece, g_ref.at[half * NCOL + q], ps.at[0], pr.at[0], swap)
    keep = pltpu.make_async_copy(piece, g_ref.at[p], lsem.at[0])

    @pl.when(jnp.logical_not(fixed))
    def _():
        out.start()

    @pl.when(fixed)
    def _():
        keep.start()

    def ring(a, t, src_up, src_down):
        zz = zh if a == 0 else 1 - zh
        if src_up is not None:
            at = zz * NY + (y + NY - t) % NY
            send(src_up, c_ref.at[at], cus.at[a * 4 + t], cur.at[a * 4 + t], up)
        if src_down is not None:
            at = zz * NY + (y + t) % NY
            send(src_down, c_ref.at[at], cds.at[a * 4 + t], cdr.at[a * 4 + t], down)

    def ring_up_wait(a, t):
        zz = zh if a == 0 else 1 - zh
        got = c_ref.at[zz * NY + (y + NY - 1 - t) % NY]
        rcopy(got, got, cus.at[a * 4 + t], cur.at[a * 4 + t], up).wait_recv()
        if t + 1 < UPS[a]:
            ring(a, t + 1, got, None)

    def ring_down_wait(a, t):
        zz = zh if a == 0 else 1 - zh
        got = c_ref.at[zz * NY + (y + 1 + t) % NY]
        rcopy(got, got, cds.at[a * 4 + t], cdr.at[a * 4 + t], down).wait_recv()
        if t + 1 < DOWNS[a]:
            ring(a, t + 1, None, got)

    send(mine, c_ref.at[q], chs.at[0], chr_.at[0], far)
    ring(0, 0, mine, mine)

    load_s.wait()
    for s in range(SL):
        for c in range(8):
            blocks = [sv[pl.ds(r * B * 8 + c, B, stride=8), :] for r in range(RC)]
            sub8[s * B : (s + 1) * B, c * B : (c + 1) * B] = pick(blocks, local[s])

    def ring_wait(a, t):
        if t < UPS[a]:
            ring_up_wait(a, t)
        if t < DOWNS[a]:
            ring_down_wait(a, t)

    ring_wait(0, 0)
    ring_wait(0, 1)
    other = c_ref.at[(1 - zh) * NY + y]
    rcopy(other, other, chs.at[0], chr_.at[0], far).wait_recv()
    ring(1, 0, other, other)

    @pl.when(jnp.logical_not(fixed))
    def _():
        rcopy(piece, g_ref.at[p], ps.at[0], pr.at[0], swap).wait_recv()

    @pl.when(fixed)
    def _():
        keep.wait()

    def fan(src, dz):
        got = g_ref.at[src]
        for d in (2, 1, 3) if dz == 2 else (1, 3):
            send(got, got, gxs.at[dz * 3 + d - 1], gxr.at[dz * 3 + d - 1], xk[d, 0])
        send(got, got, gks.at[dz * 4], gkr.at[dz * 4], core)

    own = g_ref.at[p]
    for d in (1, 3, 2):
        send(own, own, gzs.at[d - 1], gzr.at[d - 1], lzdev[d])
    fan(p, 0)

    def z_wait(d):
        src = row_id(x, (zl + NZL - d) % NZL, k)
        got = g_ref.at[src]
        rcopy(got, got, gzs.at[d - 1], gzr.at[d - 1], lzdev[d]).wait_recv()
        fan(src, d)

    def x_wait(dz, d):
        src = row_id((x + NX - d) % NX, (zl + NZL - dz) % NZL, k)
        got = g_ref.at[src]
        n = dz * 3 + d - 1
        rcopy(got, got, gxs.at[n], gxr.at[n], xk[d, 0]).wait_recv()
        n = dz * 3 + 1
        if (dz, d) in ((0, 1), (1, 3), (3, 3)):
            send(got, got, gxs.at[n], gxr.at[n], xk[d, 0])
        send(got, got, gks.at[dz * 4 + d], gkr.at[dz * 4 + d], core)

    ring_wait(0, 2)
    ring_wait(1, 0)
    z_wait(1)
    z_wait(3)
    x_wait(0, 1)
    x_wait(0, 3)
    ring_wait(1, 1)
    z_wait(2)
    x_wait(0, 2)
    ring_wait(0, 3)
    x_wait(1, 1)
    x_wait(1, 3)
    x_wait(3, 1)
    x_wait(3, 3)

    ring_wait(1, 2)

    def heard(slot):
        tile = g_ref[slot, 0:8, 2 * ROWS : 2 * ROWS + 128]
        return [jnp.max(jnp.where(tags[0:8] == t, tile, 0.0)) for t in range(SL)]

    ours, theirs = heard(p), heard(row_id((x + 2) % NX, zl, k))
    for h in range(2):
        for t in range(SL):
            which = jnp.where(half == h, ours[t], theirs[t])
            for s in range(SL):
                at = slice(s * B, (s + 1) * B)
                n = h * SL + t
                value = sub8[at, h * B : (h + 1) * B]
                for r in range(1, RC):
                    block = sub8[at, (2 * r + h) * B : (2 * r + h + 1) * B]
                    value = jnp.where(which > r - 0.5, block, value)
                sub[at, n * B : (n + 1) * B] = value

    x_wait(1, 2)
    x_wait(3, 2)
    x_wait(2, 1)
    x_wait(2, 3)
    x_wait(2, 2)
    for dz in (0, 1, 3, 2):
        for d in (0, 1, 3, 2):
            src = row_id((x + NX - d) % NX, (zl + NZL - dz) % NZL, 1 - k)
            got = g_ref.at[src]
            rcopy(got, got, gks.at[dz * 4 + d], gkr.at[dz * 4 + d], core).wait_recv()

    def panel(h, at):
        return halves(g_ref[h * NCOL : (h + 1) * NCOL, :, at : at + ROWS].reshape(W, ROWS))

    gp = [panel(h, 0) for h in range(2)]
    gq = [panel(h, ROWS) for h in range(2)]
    for s in range(SL):
        at = slice(s * B, (s + 1) * B)
        left = [halves(sub[at, h * ROWS : (h + 1) * ROWS]) for h in range(2)]
        yv[at, :] = dot3(left[0], gp[0], NT) + dot3(left[1], gp[1], NT)
        zv[at, :] = dot3(left[0], gq[0], NT) + dot3(left[1], gq[1], NT)
    ring_wait(1, 3)
    topf = c_ref[:, :, 0:W].reshape(W, W)
    top = halves(topf)
    rows = lax.broadcasted_iota(jnp.int32, (B, 1), 0)
    for s in range(SL):
        at = slice(s * B, (s + 1) * B)
        yy = jnp.where(rows < psz[s], -yv[at, :], 0.0)
        zz = jnp.where(rows < csz[s], -(zv[at, :] + dot3(halves(yy), top, NN)), 0.0)
        yv[at, :] = yy
        zv[at, :] = zz
        yz[:, :, s * CB : (s + 1) * CB, 0:W] = yy.reshape(NZH, NY, CB, W)
        yz[:, :, s * CB : (s + 1) * CB, W : 2 * W] = zz.reshape(NZH, NY, CB, W)

    def sum_up(a, t):
        n = a * 4 + t
        dst = ubuf.at[n]
        if t == 0:
            src = yz.at[a, (y + UPS[a]) % NY]
        else:
            src = ubuf.at[n - 1]
            rcopy(src, src, us.at[n - 1], ur.at[n - 1], up).wait_recv()
            ubuf[n - 1] = ubuf[n - 1] + yz[a, (y + UPS[a] - t) % NY]
        send(src, dst, us.at[n], ur.at[n], up)

    def sum_down(a, t):
        n = a * 4 + t
        dst = dbuf.at[n]
        if t == 0:
            src = yz.at[a, (y + NY - DOWNS[a]) % NY]
        else:
            src = dbuf.at[n - 1]
            rcopy(src, src, ds.at[n - 1], dr.at[n - 1], down).wait_recv()
            dbuf[n - 1] = dbuf[n - 1] + yz[a, (y + NY - DOWNS[a] + t) % NY]
        send(src, dst, ds.at[n], dr.at[n], down)

    def sum_step(t):
        for a in range(2):
            if t < UPS[a]:
                sum_up(a, t)
            if t < DOWNS[a]:
                sum_down(a, t)

    sum_step(0)

    def put(m, mat):
        for n in range(2):
            aue[n, m] = mat[:, n * 128 : (n + 1) * 128]
        send(aue.at[1 - k, m], kbuf.at[m], ks.at[m], kr.at[m], core)

    pp = halves(c_ref[:, :, W : W + ROWS].reshape(W, ROWS))
    qp = halves(c_ref[:, :, W + ROWS : OWN].reshape(W, ROWS))
    ysp = halves(yv[...])
    a_mat = dot3(pp, ysp, NN)
    put(0, a_mat)
    uv[...] = dot3(halves(a_mat), top, NN) - dot3(qp, ysp, NN).T
    first = jnp.where(p == 0, 1.0, 0.0)
    mid = pl.ds(pl.multiple_of(q * SHARE, SHARE), SHARE)
    uv[mid, :] = uv[mid, :] - first * dot3(halves(d_ref[...]), top, NN)
    u_mat = uv[...]
    put(1, u_mat)
    sum_step(1)
    e_mat = -dot3(halves(topf.T), halves(u_mat), NN) - dot3(qp, halves(zv[...]), NN)
    put(2, e_mat)

    busy = x < 3
    ahead, behind = xk[1, 0], xk[3, 0]
    nxt, prv = (x + 1) % NX, (x + 3) % NX

    def xcopy(n, m, part, dev):
        return rcopy(acc.at[m, part], xbuf.at[n], xs.at[n], xr.at[n], dev)

    def landed(n, dev):
        rcopy(xbuf.at[n], xbuf.at[n], xs.at[n], xr.at[n], dev).wait_recv()

    def relay_up():
        return xcopy(0, (x + 2) % NX, 1, ahead)

    def relay_down():
        return xcopy(1, (x + 2) % NX, 0, behind)

    def plain_up():
        return xcopy(2, nxt, 0, ahead)

    def plain_down():
        return xcopy(3, prv, 1, behind)

    def total_up():
        return xcopy(4, nxt, 1, ahead)

    def total_down():
        return xcopy(5, prv, 0, behind)

    def merge(m):
        got = kbuf.at[m]
        rcopy(got, got, ks.at[m], kr.at[m], core).wait_recv()
        acc[m] = (aue[k, m] + kbuf[m]).reshape(2, 128, 128)

    opposite = (x + 2) % NX

    @pl.when(opposite < 3)
    def _():
        merge(opposite)
        relay_up().start()
        relay_down().start()

    @pl.when(nxt < 3)
    def _():
        merge(nxt)
        plain_up().start()

    @pl.when(prv < 3)
    def _():
        merge(prv)
        plain_down().start()

    @pl.when(busy)
    def _():
        merge(x)

    sum_step(2)

    @pl.when(nxt < 3)
    def _():
        landed(0, ahead)
        acc[nxt, 1] = acc[nxt, 1] + xbuf[0]
        total_up().start()

    @pl.when(prv < 3)
    def _():
        landed(1, behind)
        acc[prv, 0] = acc[prv, 0] + xbuf[1]
        total_down().start()

    sum_step(3)

    def ycopy(d):
        return rcopy(accx.at[:, (y + d) % NY], ybuf.at[d - 1], ys.at[d - 1], yr.at[d - 1], ydev[d])

    def zcopy(d):
        return rcopy(accy.at[zpos[d] // NZL], zbuf.at[d - 1], zs.at[d - 1], zr.at[d - 1], zdev[d])

    def fcopy(d, f):
        n = d * 2 + f - 1
        return rcopy(auo.at[x, k], auo.at[x, k], fs.at[n], fr.at[n], xk[d, f])

    @pl.when(busy)
    def _():
        for n in range(2, 6):
            landed(n, ahead if n % 2 == 0 else behind)
        low = acc[x, 0] + (xbuf[2] + xbuf[5])
        high = acc[x, 1] + (xbuf[3] + xbuf[4])
        accx[0] = low.reshape(NY, SHARE, 128)
        accx[1] = high.reshape(NY, SHARE, 128)
        for d in (4, 3, 5, 2, 6, 1, 7):
            ycopy(d).start()

    for a in range(2):
        n = a * 4 + UPS[a] - 1
        got = ubuf.at[n]
        rcopy(got, got, us.at[n], ur.at[n], up).wait_recv()
        n2 = a * 4 + DOWNS[a] - 1
        got = dbuf.at[n2]
        rcopy(got, got, ds.at[n2], dr.at[n2], down).wait_recv()
        yzacc[a] = yz[a, y] + (ubuf[n] + dbuf[n2])
    send(yzacc.at[1 - zh], hbuf, hs.at[0], hr.at[0], far)

    hop = rcopy(hbuf, hbuf, hs.at[0], hr.at[0], far)
    @pl.when(busy)
    def _():
        for d in range(1, NY):
            ycopy(d).wait_recv()
        total = accx[:, y]
        for d in range(NY - 1):
            total = total + ybuf[d]
        accy[...] = total
        for d in (4, 3, 5, 2, 6, 1, 7):
            zcopy(d).start()

    hop.wait_recv()
    yzo[...] = yzacc[zh] + hbuf[...]

    @pl.when(busy)
    def _():
        for d in range(1, NZ):
            zcopy(d).wait_recv()
        total = accy[zh]
        for d in range(NZ - 1):
            total = total + zbuf[d]
        auo[x, k] = total
        for d, f in xk:
            fcopy(d, f).start()

    for d, f in xk:
        m = (x + NX - d) % NX
        n = d * 2 + f - 1

        @pl.when(m < 3)
        def _():
            got = auo.at[m, k if f == 0 else 1 - k]
            rcopy(got, got, fs.at[n], fr.at[n], xk[d, f]).wait_recv()

    @pl.when(jnp.logical_not(fixed))
    def _():
        out.wait_send()

    for copy in sends:
        copy.wait_send()

    @pl.when((x + 2) % NX < 3)
    def _():
        relay_up().wait_send()
        relay_down().wait_send()

    @pl.when(nxt < 3)
    def _():
        plain_up().wait_send()
        total_up().wait_send()

    @pl.when(prv < 3)
    def _():
        plain_down().wait_send()
        total_down().wait_send()

    @pl.when(busy)
    def _():
        for d in range(1, NY):
            ycopy(d).wait_send()
        for d in range(1, NZ):
            zcopy(d).wait_send()
        for d, f in xk:
            fcopy(d, f).wait_send()


def step(*operands):
    vmem = pl.BlockSpec(memory_space=pltpu.VMEM)
    dma = pltpu.SemaphoreType.DMA
    rows = SL * CB
    buffers = [
        (SL, SHARE, B),
        (SL, SHARE, B),
        (SHARE, W),
        (RC * B * 8, B),
        (ROWS, 8 * B),
        (ROWS, 2 * ROWS),
        (SHARE, WIDE),
        (NROW, SHARE, PATCH),
        (NCOL, SHARE, OWN),
        (ROWS, W),
        (ROWS, W),
        (W, W),
        (NZH, NY, rows, 2 * W),
        (2, 3, W, 128),
        (3, W, 128),
        (3, 2, 128, 128),
        (6, 128, 128),
        (NZH, NY, SHARE, 128),
        (NY - 1, NZH, SHARE, 128),
        (NZH, SHARE, 128),
        (NZ - 1, SHARE, 128),
        (8, rows, 2 * W),
        (8, rows, 2 * W),
        (NZH, rows, 2 * W),
        (rows, 2 * W),
    ]
    sems = [1, 7, 1, 1, 1, 3, 3, 12, 12, 16, 16, 1, 1, 8, 8, 8, 8]
    sems += [3, 3, 6, 6, 7, 7, 7, 7, 7, 7, 8, 8, 8, 8, 1, 1]
    return pl.pallas_call(
        step_kernel,
        out_shape=(
            jax.ShapeDtypeStruct((rows, 2 * W), F32),
            jax.ShapeDtypeStruct((3, 2, SHARE, 128), F32),
        ),
        in_specs=[pl.BlockSpec(memory_space=pl.ANY)] * 8,
        out_specs=(vmem, vmem),
        scratch_shapes=[pltpu.SMEM((SL,), jnp.int32)] * 3
        + [pltpu.VMEM(b, F32) for b in buffers]
        + [dma((n,)) for n in sems],
        compiler_params=pltpu.CompilerParams(collective_id=0, has_side_effects=True),
        name="step",
    )(*operands)


def place_kernel(pb, yz_ref, mats_ref, d_ref, cd_ref, prow, pd, crow, cu, cdiag):
    p = lax.axis_index("row")
    for r in range(RC):
        ya = jnp.zeros((CB, W), F32)
        za = jnp.zeros((CB, W), F32)
        for s in range(SL):
            here = pb[s] == r * NROW + p
            ya = jnp.where(here, yz_ref[s * CB : (s + 1) * CB, 0:W], ya)
            za = jnp.where(here, yz_ref[s * CB : (s + 1) * CB, W:], za)
        prow[r] = ya
        crow[r] = za
    for n in range(2):
        at = slice(n * 128, (n + 1) * 128)
        pd[:, at] = d_ref[:, at] - mats_ref[0, n]
        cu[:, at] = mats_ref[1, n]
        cdiag[:, at] = cd_ref[:, at] + mats_ref[2, n]


def lay(*operands):
    vmem = pl.BlockSpec(memory_space=pltpu.VMEM)
    smem = pl.BlockSpec(memory_space=pltpu.SMEM)
    share = jax.ShapeDtypeStruct((SHARE, W), F32)
    rows = jax.ShapeDtypeStruct((RC, CB, W), F32)
    return pl.pallas_call(
        place_kernel,
        out_shape=(rows, share, rows, share, share),
        in_specs=[smem] + [vmem] * 4,
        out_specs=(vmem,) * 5,
        name="lay",
    )(*operands)


def body(
    cached_inverse,
    parent_panel,
    parent_blocks,
    parent_sizes,
    parent_diagonal,
    child_panel,
    child_top,
    child_blocks,
    child_sizes,
    child_diagonal,
):
    rows, mats = step(
        parent_blocks,
        parent_sizes,
        child_sizes,
        cached_inverse.reshape(RC * B * 8, B),
        jnp.transpose(parent_panel, (1, 0, 2)),
        jnp.transpose(child_panel, (1, 0, 2)),
        child_top,
        parent_diagonal,
    )
    prow, pd, crow, cu, cdiag = lay(parent_blocks, rows, mats, parent_diagonal, child_diagonal)
    return (prow[:, None], pd, crow[:, None], cu, cdiag)


def solution(mesh):
    in_specs = (
        P(None, "row", None, None, "col", None),
        P("col", "row", None),
        P("row"),
        P("row"),
        P("col", None),
        P("col", "row", None),
        P("col", None),
        P("row"),
        P("row"),
        P("col", None),
    )
    out_specs = (
        P(None, "row", "col", None),
        P("col", None),
        P(None, "row", "col", None),
        P("col", None),
        P("col", None),
    )
    return jax.shard_map(body, mesh=mesh, in_specs=in_specs, out_specs=out_specs, check_vma=False)
```

```python
import jax
import jax.numpy as jnp
from jax import lax
from jax.experimental import pallas as pl
from jax.experimental.pallas import tpu as pltpu
from jax.sharding import PartitionSpec as P

MESH = pl.DeviceIdType.MESH
F32 = jnp.float32
BF16 = jnp.bfloat16

NX, NZL, NZH, NY, NK = 4, 4, 2, 8, 2
NZ = NZL * NZH
NROW, NCOL = NX * NZL * NK, NZH * NY
W, B, SL, RC = 256, 128, 3, 4
SHARE = W // NCOL
ROWS = SL * B
CB = B // NCOL
PATCH = 2 * ROWS
OWN = W + PATCH
UPS = (4, 3)
DOWNS = (3, 4)


def place():
    p = lax.axis_index("row")
    q = lax.axis_index("col")
    x = p // (NZL * NK)
    zl = (p // NK) % NZL
    k = p % NK
    return p, q, x, zl, k, q // NY, q % NY


def row_id(x, zl, k):
    return (x * NZL + zl) * NK + k


def rcopy(src, dst, send, recv, target):
    return pltpu.make_async_remote_copy(
        src_ref=src,
        dst_ref=dst,
        send_sem=send,
        recv_sem=recv,
        device_id=target,
        device_id_type=MESH,
    )


def halves(a):
    hi = a.astype(BF16)
    lo = (a - hi.astype(F32)).astype(BF16)
    return hi, lo


def dot3(a, b, dims):
    def one(u, v):
        return lax.dot_general(u, v, (dims, ((), ())), preferred_element_type=F32)

    return one(a[0], b[0]) + (one(a[0], b[1]) + one(a[1], b[0]))


NN = ((1,), (0,))
NT = ((1,), (1,))


def pick(values, which, first=0):
    out = values[0]
    for n in range(1, len(values)):
        out = jnp.where(which == n, values[n], out)
    return out


def step_kernel(
    pb_hbm, psz_hbm, csz_hbm, s_hbm, pp_hbm, cp_hbm, top_hbm, d_hbm,
    yzo, auo,
    pb, psz, csz, pp_ref, cp_ref, d_ref, sv, sub8, sub, xv, told, heard, g_ref, c_ref, yv, zv, uv, yz, aue,
    kbuf, acc, xbuf, accx, ybuf, accy, zbuf, ubuf, dbuf, yzacc, hbuf,
    ssem, isem, ps, pr, lsem, gzs, gzr, gxs, gxr, gks, gkr, chs, chr_, cus, cur, cds, cdr,
    ks, kr, xs, xr, ys, yr, zs, zr, fs, fr, us, ur, ds, dr, hs, hr,
):
    p, q, x, zl, k, zh, y = place()
    z = zh * NZL + zl
    half, cls = p // NCOL, p % NCOL
    fixed = q == cls
    swap = (half * NCOL + q, cls)
    xk = {}
    for d in range(NX):
        for f in range(2):
            if d or f:
                xk[d, f] = (row_id((x + d) % NX, zl, k if f == 0 else 1 - k), q)
    core = xk[0, 1]
    lzdev = [None] + [(row_id(x, (zl + d) % NZL, k), q) for d in range(1, NZL)]
    ydev = [None] + [(p, zh * NY + (y + d) % NY) for d in range(1, NY)]
    up, down = ydev[1], ydev[NY - 1]
    zpos = [(z + d) % NZ for d in range(NZ)]
    zdev = [None] + [(row_id(x, zpos[d] % NZL, k), (zpos[d] // NZL) * NY + y) for d in range(1, NZ)]
    far = zdev[NZL]

    barrier = pltpu.get_barrier_semaphore()

    @pl.when(jnp.logical_not(fixed))
    def _():
        pl.semaphore_signal(barrier, inc=1, device_id=swap, device_id_type=MESH)

    for dev in zdev[1:] + ydev[1:] + list(xk.values()):
        pl.semaphore_signal(barrier, inc=1, device_id=dev, device_id_type=MESH)

    loads = [
        pltpu.make_async_copy(src, dst, isem.at[n])
        for n, (src, dst) in enumerate((
            (psz_hbm, psz),
            (csz_hbm, csz),
            (pb_hbm, pb),
            (pp_hbm, pp_ref),
            (cp_hbm, cp_ref),
            (top_hbm, xv.at[:, 0:W]),
            (d_hbm, d_ref),
        ))
    ]
    for load in loads:
        load.start()
    load_s = pltpu.make_async_copy(s_hbm, sv, ssem.at[0])
    load_s.start()
    for load in loads:
        load.wait()

    lane = lax.broadcasted_iota(jnp.int32, (SHARE, B), 1)
    for s in range(SL):
        at = W + s * B
        xv[:, at : at + B] = jnp.where(lane < psz[s], pp_ref[s], 0.0)
        at += ROWS
        xv[:, at : at + B] = jnp.where(lane < csz[s], cp_ref[s], 0.0)
    local = [jnp.maximum(pb[s], 0) // NROW for s in range(SL)]
    tag = jnp.zeros((SHARE, 128), F32)
    tags = lax.broadcasted_iota(jnp.int32, (SHARE, 128), 1)
    for s in range(SL):
        tag = jnp.where(tags == s, local[s].astype(F32), tag)
    told[...] = tag[0:8]
    c_ref[q] = xv[...]

    pl.semaphore_wait(barrier, 7 + NY - 1 + NZ - 1 + jnp.where(fixed, 0, 1))

    sends = []

    def send(*args):
        copy = rcopy(*args)
        copy.start()
        sends.append(copy)

    piece = xv.at[:, W:OWN]
    mine = xv
    out = rcopy(piece, g_ref.at[half * NCOL + q], ps.at[0], pr.at[0], swap)
    keep = pltpu.make_async_copy(piece, g_ref.at[p], lsem.at[0])
    out_tag = rcopy(told, heard.at[0], ps.at[1], pr.at[1], swap)
    keep_tag = pltpu.make_async_copy(told, heard.at[0], lsem.at[1])

    @pl.when(jnp.logical_not(fixed))
    def _():
        out.start()
        out_tag.start()

    @pl.when(fixed)
    def _():
        keep.start()
        keep_tag.start()

    def ring(a, t, src_up, src_down):
        zz = zh if a == 0 else 1 - zh
        if src_up is not None:
            at = zz * NY + (y + NY - t) % NY
            send(src_up, c_ref.at[at], cus.at[a * 4 + t], cur.at[a * 4 + t], up)
        if src_down is not None:
            at = zz * NY + (y + t) % NY
            send(src_down, c_ref.at[at], cds.at[a * 4 + t], cdr.at[a * 4 + t], down)

    def ring_up_wait(a, t):
        zz = zh if a == 0 else 1 - zh
        got = c_ref.at[zz * NY + (y + NY - 1 - t) % NY]
        rcopy(got, got, cus.at[a * 4 + t], cur.at[a * 4 + t], up).wait_recv()
        if t + 1 < UPS[a]:
            ring(a, t + 1, got, None)

    def ring_down_wait(a, t):
        zz = zh if a == 0 else 1 - zh
        got = c_ref.at[zz * NY + (y + 1 + t) % NY]
        rcopy(got, got, cds.at[a * 4 + t], cdr.at[a * 4 + t], down).wait_recv()
        if t + 1 < DOWNS[a]:
            ring(a, t + 1, None, got)

    send(mine, c_ref.at[q], chs.at[0], chr_.at[0], far)
    ring(0, 0, mine, mine)

    load_s.wait()
    for s in range(SL):
        for c in range(8):
            blocks = [sv[pl.ds(r * B * 8 + c, B, stride=8), :] for r in range(RC)]
            sub8[s * B : (s + 1) * B, c * B : (c + 1) * B] = pick(blocks, local[s])

    def ring_wait(a, t):
        if t < UPS[a]:
            ring_up_wait(a, t)
        if t < DOWNS[a]:
            ring_down_wait(a, t)

    ring_wait(0, 0)
    ring_wait(0, 1)
    other = c_ref.at[(1 - zh) * NY + y]
    rcopy(other, other, chs.at[0], chr_.at[0], far).wait_recv()
    ring(1, 0, other, other)

    @pl.when(jnp.logical_not(fixed))
    def _():
        rcopy(piece, g_ref.at[p], ps.at[0], pr.at[0], swap).wait_recv()
        out_tag.wait_recv()

    @pl.when(fixed)
    def _():
        keep.wait()
        keep_tag.wait()

    def fan(src, dz):
        got = g_ref.at[src]
        for d in (2, 1, 3) if dz == 2 else (1, 3):
            send(got, got, gxs.at[dz * 3 + d - 1], gxr.at[dz * 3 + d - 1], xk[d, 0])
        send(got, got, gks.at[dz * 4], gkr.at[dz * 4], core)

    own = g_ref.at[p]
    for d in (1, 3, 2):
        send(own, own, gzs.at[d - 1], gzr.at[d - 1], lzdev[d])
    fan(p, 0)
    send(heard.at[0], heard.at[1], gxs.at[12], gxr.at[12], xk[2, 0])

    def z_wait(d):
        src = row_id(x, (zl + NZL - d) % NZL, k)
        got = g_ref.at[src]
        rcopy(got, got, gzs.at[d - 1], gzr.at[d - 1], lzdev[d]).wait_recv()
        fan(src, d)

    def x_wait(dz, d):
        src = row_id((x + NX - d) % NX, (zl + NZL - dz) % NZL, k)
        got = g_ref.at[src]
        n = dz * 3 + d - 1
        rcopy(got, got, gxs.at[n], gxr.at[n], xk[d, 0]).wait_recv()
        n = dz * 3 + 1
        if (dz, d) in ((0, 1), (1, 3), (3, 3)):
            send(got, got, gxs.at[n], gxr.at[n], xk[d, 0])
        send(got, got, gks.at[dz * 4 + d], gkr.at[dz * 4 + d], core)

    ring_wait(0, 2)
    z_wait(1)
    z_wait(3)
    x_wait(0, 1)
    x_wait(0, 3)
    ring_wait(1, 0)
    z_wait(2)
    x_wait(0, 2)
    ring_wait(0, 3)
    x_wait(1, 1)
    x_wait(1, 3)
    ring_wait(1, 1)
    x_wait(3, 1)
    x_wait(3, 3)
    x_wait(1, 2)
    x_wait(3, 2)
    x_wait(2, 1)
    x_wait(2, 3)
    ring_wait(1, 2)
    x_wait(2, 2)

    rcopy(heard.at[1], heard.at[1], gxs.at[12], gxr.at[12], xk[2, 0]).wait_recv()
    said = [[jnp.max(jnp.where(tags[0:8] == t, heard[h], 0.0)) for t in range(SL)] for h in range(2)]
    for h in range(2):
        for t in range(SL):
            which = jnp.where(half == h, said[0][t], said[1][t])
            for s in range(SL):
                at = slice(s * B, (s + 1) * B)
                n = h * SL + t
                value = sub8[at, h * B : (h + 1) * B]
                for r in range(1, RC):
                    block = sub8[at, (2 * r + h) * B : (2 * r + h + 1) * B]
                    value = jnp.where(which > r - 0.5, block, value)
                sub[at, n * B : (n + 1) * B] = value

    for dz in (0, 1, 3, 2):
        for d in (0, 1, 3, 2):
            src = row_id((x + NX - d) % NX, (zl + NZL - dz) % NZL, 1 - k)
            got = g_ref.at[src]
            rcopy(got, got, gks.at[dz * 4 + d], gkr.at[dz * 4 + d], core).wait_recv()

    def panel(h, at):
        return halves(g_ref[h * NCOL : (h + 1) * NCOL, :, at : at + ROWS].reshape(W, ROWS))

    gp = [panel(h, 0) for h in range(2)]
    gq = [panel(h, ROWS) for h in range(2)]
    for s in range(SL):
        at = slice(s * B, (s + 1) * B)
        left = [halves(sub[at, h * ROWS : (h + 1) * ROWS]) for h in range(2)]
        yv[at, :] = dot3(left[0], gp[0], NT) + dot3(left[1], gp[1], NT)
        zv[at, :] = dot3(left[0], gq[0], NT) + dot3(left[1], gq[1], NT)
    ring_wait(1, 3)
    topf = c_ref[:, :, 0:W].reshape(W, W)
    top = halves(topf)
    rows = lax.broadcasted_iota(jnp.int32, (B, 1), 0)
    for s in range(SL):
        at = slice(s * B, (s + 1) * B)
        yy = jnp.where(rows < psz[s], -yv[at, :], 0.0)
        zz = jnp.where(rows < csz[s], -(zv[at, :] + dot3(halves(yy), top, NN)), 0.0)
        yv[at, :] = yy
        zv[at, :] = zz
        yz[:, :, s * CB : (s + 1) * CB, 0:W] = yy.reshape(NZH, NY, CB, W)
        yz[:, :, s * CB : (s + 1) * CB, W : 2 * W] = zz.reshape(NZH, NY, CB, W)

    def sum_up(a, t):
        n = a * 4 + t
        dst = ubuf.at[n]
        if t == 0:
            src = yz.at[a, (y + UPS[a]) % NY]
        else:
            src = ubuf.at[n - 1]
            rcopy(src, src, us.at[n - 1], ur.at[n - 1], up).wait_recv()
            ubuf[n - 1] = ubuf[n - 1] + yz[a, (y + UPS[a] - t) % NY]
        send(src, dst, us.at[n], ur.at[n], up)

    def sum_down(a, t):
        n = a * 4 + t
        dst = dbuf.at[n]
        if t == 0:
            src = yz.at[a, (y + NY - DOWNS[a]) % NY]
        else:
            src = dbuf.at[n - 1]
            rcopy(src, src, ds.at[n - 1], dr.at[n - 1], down).wait_recv()
            dbuf[n - 1] = dbuf[n - 1] + yz[a, (y + NY - DOWNS[a] + t) % NY]
        send(src, dst, ds.at[n], dr.at[n], down)

    def sum_step(t):
        for a in range(2):
            if t < UPS[a]:
                sum_up(a, t)
            if t < DOWNS[a]:
                sum_down(a, t)

    sum_step(0)

    def put(m, mat):
        for n in range(2):
            aue[n, m] = mat[:, n * 128 : (n + 1) * 128]
        send(aue.at[1 - k, m], kbuf.at[m], ks.at[m], kr.at[m], core)

    pp = halves(c_ref[:, :, W : W + ROWS].reshape(W, ROWS))
    qp = halves(c_ref[:, :, W + ROWS : OWN].reshape(W, ROWS))
    ysp = halves(yv[...])
    a_mat = dot3(pp, ysp, NN)
    put(0, a_mat)
    uv[...] = dot3(halves(a_mat), top, NN) - dot3(qp, ysp, NN).T
    first = jnp.where(p == 0, 1.0, 0.0)
    mid = pl.ds(pl.multiple_of(q * SHARE, SHARE), SHARE)
    uv[mid, :] = uv[mid, :] - first * dot3(halves(d_ref[...]), top, NN)
    u_mat = uv[...]
    put(1, u_mat)
    e_mat = -dot3(halves(topf.T), halves(u_mat), NN) - dot3(qp, halves(zv[...]), NN)
    put(2, e_mat)

    busy = x < 3
    ahead, behind = xk[1, 0], xk[3, 0]
    nxt, prv = (x + 1) % NX, (x + 3) % NX

    def xcopy(n, m, part, dev):
        return rcopy(acc.at[m, part], xbuf.at[n], xs.at[n], xr.at[n], dev)

    def landed(n, dev):
        rcopy(xbuf.at[n], xbuf.at[n], xs.at[n], xr.at[n], dev).wait_recv()

    def relay_up():
        return xcopy(0, (x + 2) % NX, 1, ahead)

    def relay_down():
        return xcopy(1, (x + 2) % NX, 0, behind)

    def plain_up():
        return xcopy(2, nxt, 0, ahead)

    def plain_down():
        return xcopy(3, prv, 1, behind)

    def total_up():
        return xcopy(4, nxt, 1, ahead)

    def total_down():
        return xcopy(5, prv, 0, behind)

    def merge(m):
        got = kbuf.at[m]
        rcopy(got, got, ks.at[m], kr.at[m], core).wait_recv()
        acc[m] = (aue[k, m] + kbuf[m]).reshape(2, 128, 128)

    opposite = (x + 2) % NX

    @pl.when(opposite < 3)
    def _():
        merge(opposite)
        relay_up().start()
        relay_down().start()

    @pl.when(nxt < 3)
    def _():
        merge(nxt)
        plain_up().start()

    @pl.when(prv < 3)
    def _():
        merge(prv)
        plain_down().start()

    @pl.when(busy)
    def _():
        merge(x)

    sum_step(1)
    sum_step(2)

    @pl.when(nxt < 3)
    def _():
        landed(0, ahead)
        acc[nxt, 1] = acc[nxt, 1] + xbuf[0]
        total_up().start()

    @pl.when(prv < 3)
    def _():
        landed(1, behind)
        acc[prv, 0] = acc[prv, 0] + xbuf[1]
        total_down().start()

    sum_step(3)

    def ycopy(d):
        return rcopy(accx.at[:, (y + d) % NY], ybuf.at[d - 1], ys.at[d - 1], yr.at[d - 1], ydev[d])

    def zcopy(d):
        return rcopy(accy.at[zpos[d] // NZL], zbuf.at[d - 1], zs.at[d - 1], zr.at[d - 1], zdev[d])

    def fcopy(d, f):
        n = d * 2 + f - 1
        return rcopy(auo.at[x, k], auo.at[x, k], fs.at[n], fr.at[n], xk[d, f])

    @pl.when(busy)
    def _():
        for n in range(2, 6):
            landed(n, ahead if n % 2 == 0 else behind)
        low = acc[x, 0] + (xbuf[2] + xbuf[5])
        high = acc[x, 1] + (xbuf[3] + xbuf[4])
        accx[0] = low.reshape(NY, SHARE, 128)
        accx[1] = high.reshape(NY, SHARE, 128)
        for d in (4, 3, 5, 2, 6, 1, 7):
            ycopy(d).start()

    for a in range(2):
        n = a * 4 + UPS[a] - 1
        got = ubuf.at[n]
        rcopy(got, got, us.at[n], ur.at[n], up).wait_recv()
        n2 = a * 4 + DOWNS[a] - 1
        got = dbuf.at[n2]
        rcopy(got, got, ds.at[n2], dr.at[n2], down).wait_recv()
        yzacc[a] = yz[a, y] + (ubuf[n] + dbuf[n2])
    send(yzacc.at[1 - zh], hbuf, hs.at[0], hr.at[0], far)

    hop = rcopy(hbuf, hbuf, hs.at[0], hr.at[0], far)
    @pl.when(busy)
    def _():
        for d in range(1, NY):
            ycopy(d).wait_recv()
        total = accx[:, y]
        for d in range(NY - 1):
            total = total + ybuf[d]
        accy[...] = total
        for d in (4, 3, 5, 2, 6, 1, 7):
            zcopy(d).start()

    hop.wait_recv()
    yzo[...] = yzacc[zh] + hbuf[...]

    @pl.when(busy)
    def _():
        for d in range(1, NZ):
            zcopy(d).wait_recv()
        total = accy[zh]
        for d in range(NZ - 1):
            total = total + zbuf[d]
        auo[x, k] = total
        for d, f in xk:
            fcopy(d, f).start()

    for d, f in xk:
        m = (x + NX - d) % NX
        n = d * 2 + f - 1

        @pl.when(m < 3)
        def _():
            got = auo.at[m, k if f == 0 else 1 - k]
            rcopy(got, got, fs.at[n], fr.at[n], xk[d, f]).wait_recv()

    @pl.when(jnp.logical_not(fixed))
    def _():
        out.wait_send()
        out_tag.wait_send()

    for copy in sends:
        copy.wait_send()

    @pl.when((x + 2) % NX < 3)
    def _():
        relay_up().wait_send()
        relay_down().wait_send()

    @pl.when(nxt < 3)
    def _():
        plain_up().wait_send()
        total_up().wait_send()

    @pl.when(prv < 3)
    def _():
        plain_down().wait_send()
        total_down().wait_send()

    @pl.when(busy)
    def _():
        for d in range(1, NY):
            ycopy(d).wait_send()
        for d in range(1, NZ):
            zcopy(d).wait_send()
        for d, f in xk:
            fcopy(d, f).wait_send()


def step(*operands):
    vmem = pl.BlockSpec(memory_space=pltpu.VMEM)
    dma = pltpu.SemaphoreType.DMA
    rows = SL * CB
    buffers = [
        (SL, SHARE, B),
        (SL, SHARE, B),
        (SHARE, W),
        (RC * B * 8, B),
        (ROWS, 8 * B),
        (ROWS, 2 * ROWS),
        (SHARE, OWN),
        (8, 128),
        (2, 8, 128),
        (NROW, SHARE, PATCH),
        (NCOL, SHARE, OWN),
        (ROWS, W),
        (ROWS, W),
        (W, W),
        (NZH, NY, rows, 2 * W),
        (2, 3, W, 128),
        (3, W, 128),
        (3, 2, 128, 128),
        (6, 128, 128),
        (NZH, NY, SHARE, 128),
        (NY - 1, NZH, SHARE, 128),
        (NZH, SHARE, 128),
        (NZ - 1, SHARE, 128),
        (8, rows, 2 * W),
        (8, rows, 2 * W),
        (NZH, rows, 2 * W),
        (rows, 2 * W),
    ]
    sems = [1, 7, 2, 2, 2, 3, 3, 13, 13, 16, 16, 1, 1, 8, 8, 8, 8]
    sems += [3, 3, 6, 6, 7, 7, 7, 7, 7, 7, 8, 8, 8, 8, 1, 1]
    return pl.pallas_call(
        step_kernel,
        out_shape=(
            jax.ShapeDtypeStruct((rows, 2 * W), F32),
            jax.ShapeDtypeStruct((3, 2, SHARE, 128), F32),
        ),
        in_specs=[pl.BlockSpec(memory_space=pl.ANY)] * 8,
        out_specs=(vmem, vmem),
        scratch_shapes=[pltpu.SMEM((SL,), jnp.int32)] * 3
        + [pltpu.VMEM(b, F32) for b in buffers]
        + [dma((n,)) for n in sems],
        compiler_params=pltpu.CompilerParams(collective_id=0, has_side_effects=True),
        name="step",
    )(*operands)


def place_kernel(pb, yz_ref, mats_ref, d_ref, cd_ref, prow, pd, crow, cu, cdiag):
    p = lax.axis_index("row")
    for r in range(RC):
        ya = jnp.zeros((CB, W), F32)
        za = jnp.zeros((CB, W), F32)
        for s in range(SL):
            here = pb[s] == r * NROW + p
            ya = jnp.where(here, yz_ref[s * CB : (s + 1) * CB, 0:W], ya)
            za = jnp.where(here, yz_ref[s * CB : (s + 1) * CB, W:], za)
        prow[r] = ya
        crow[r] = za
    for n in range(2):
        at = slice(n * 128, (n + 1) * 128)
        pd[:, at] = d_ref[:, at] - mats_ref[0, n]
        cu[:, at] = mats_ref[1, n]
        cdiag[:, at] = cd_ref[:, at] + mats_ref[2, n]


def lay(*operands):
    vmem = pl.BlockSpec(memory_space=pltpu.VMEM)
    smem = pl.BlockSpec(memory_space=pltpu.SMEM)
    share = jax.ShapeDtypeStruct((SHARE, W), F32)
    rows = jax.ShapeDtypeStruct((RC, CB, W), F32)
    return pl.pallas_call(
        place_kernel,
        out_shape=(rows, share, rows, share, share),
        in_specs=[smem] + [vmem] * 4,
        out_specs=(vmem,) * 5,
        name="lay",
    )(*operands)


def body(
    cached_inverse,
    parent_panel,
    parent_blocks,
    parent_sizes,
    parent_diagonal,
    child_panel,
    child_top,
    child_blocks,
    child_sizes,
    child_diagonal,
):
    rows, mats = step(
        parent_blocks,
        parent_sizes,
        child_sizes,
        cached_inverse.reshape(RC * B * 8, B),
        jnp.transpose(parent_panel, (1, 0, 2)),
        jnp.transpose(child_panel, (1, 0, 2)),
        child_top,
        parent_diagonal,
    )
    prow, pd, crow, cu, cdiag = lay(parent_blocks, rows, mats, parent_diagonal, child_diagonal)
    return (prow[:, None], pd, crow[:, None], cu, cdiag)


def solution(mesh):
    in_specs = (
        P(None, "row", None, None, "col", None),
        P("col", "row", None),
        P("row"),
        P("row"),
        P("col", None),
        P("col", "row", None),
        P("col", None),
        P("row"),
        P("row"),
        P("col", None),
    )
    out_specs = (
        P(None, "row", "col", None),
        P("col", None),
        P(None, "row", "col", None),
        P("col", None),
        P("col", None),
    )
    return jax.shard_map(body, mesh=mesh, in_specs=in_specs, out_specs=out_specs, check_vma=False)
```

```python
import jax
import jax.numpy as jnp
from jax import lax
from jax.experimental import pallas as pl
from jax.experimental.pallas import tpu as pltpu
from jax.sharding import PartitionSpec as P

MESH = pl.DeviceIdType.MESH
F32 = jnp.float32
BF16 = jnp.bfloat16

NX, NZL, NZH, NY, NK = 4, 4, 2, 8, 2
NZ = NZL * NZH
NROW, NCOL = NX * NZL * NK, NZH * NY
W, B, SL, RC = 256, 128, 3, 4
SHARE = W // NCOL
ROWS = SL * B
CB = B // NCOL
PATCH = 2 * ROWS
OWN = W + PATCH
UPS = (4, 3)
DOWNS = (3, 4)


def place():
    p = lax.axis_index("row")
    q = lax.axis_index("col")
    x = p // (NZL * NK)
    zl = (p // NK) % NZL
    k = p % NK
    return p, q, x, zl, k, q // NY, q % NY


def row_id(x, zl, k):
    return (x * NZL + zl) * NK + k


def rcopy(src, dst, send, recv, target):
    return pltpu.make_async_remote_copy(
        src_ref=src,
        dst_ref=dst,
        send_sem=send,
        recv_sem=recv,
        device_id=target,
        device_id_type=MESH,
    )


def halves(a):
    hi = a.astype(BF16)
    lo = (a - hi.astype(F32)).astype(BF16)
    return hi, lo


def dot3(a, b, dims):
    def one(u, v):
        return lax.dot_general(u, v, (dims, ((), ())), preferred_element_type=F32)

    return one(a[0], b[0]) + (one(a[0], b[1]) + one(a[1], b[0]))


NN = ((1,), (0,))
NT = ((1,), (1,))


def pick(values, which, first=0):
    out = values[0]
    for n in range(1, len(values)):
        out = jnp.where(which == n, values[n], out)
    return out


def step_kernel(
    pb_hbm, psz_hbm, csz_hbm, s_hbm, pp_hbm, cp_hbm, top_hbm, d_hbm,
    yzo, auo,
    pb, psz, csz, pp_ref, cp_ref, d_ref, sv, sub8, sub, xv, told, heard, g_ref, c_ref, yv, zv, uv, yz, aue,
    kbuf, acc, xbuf, accx, ybuf, accy, zbuf, ubuf, dbuf, yzacc, hbuf,
    ssem, isem, ps, pr, lsem, gzs, gzr, gxs, gxr, gks, gkr, chs, chr_, cus, cur, cds, cdr, cas, car,
    ks, kr, xs, xr, ys, yr, zs, zr, fs, fr, us, ur, ds, dr, hs, hr,
):
    p, q, x, zl, k, zh, y = place()
    z = zh * NZL + zl
    half, cls = p // NCOL, p % NCOL
    fixed = q == cls
    swap = (half * NCOL + q, cls)
    xk = {}
    for d in range(NX):
        for f in range(2):
            if d or f:
                xk[d, f] = (row_id((x + d) % NX, zl, k if f == 0 else 1 - k), q)
    core = xk[0, 1]
    lzdev = [None] + [(row_id(x, (zl + d) % NZL, k), q) for d in range(1, NZL)]
    ydev = [None] + [(p, zh * NY + (y + d) % NY) for d in range(1, NY)]
    up, down = ydev[1], ydev[NY - 1]
    zpos = [(z + d) % NZ for d in range(NZ)]
    zdev = [None] + [(row_id(x, zpos[d] % NZL, k), (zpos[d] // NZL) * NY + y) for d in range(1, NZ)]
    far = zdev[NZL]

    barrier = pltpu.get_barrier_semaphore()

    @pl.when(jnp.logical_not(fixed))
    def _():
        pl.semaphore_signal(barrier, inc=1, device_id=swap, device_id_type=MESH)

    for dev in zdev[1:] + ydev[1:] + list(xk.values()):
        pl.semaphore_signal(barrier, inc=1, device_id=dev, device_id_type=MESH)

    loads = [
        pltpu.make_async_copy(src, dst, isem.at[n])
        for n, (src, dst) in enumerate((
            (psz_hbm, psz),
            (csz_hbm, csz),
            (pb_hbm, pb),
            (pp_hbm, pp_ref),
            (cp_hbm, cp_ref),
            (top_hbm, xv.at[:, 0:W]),
            (d_hbm, d_ref),
        ))
    ]
    for load in loads:
        load.start()
    load_s = pltpu.make_async_copy(s_hbm, sv, ssem.at[0])
    load_s.start()
    for load in loads:
        load.wait()

    lane = lax.broadcasted_iota(jnp.int32, (SHARE, B), 1)
    for s in range(SL):
        at = W + s * B
        xv[:, at : at + B] = jnp.where(lane < psz[s], pp_ref[s], 0.0)
        at += ROWS
        xv[:, at : at + B] = jnp.where(lane < csz[s], cp_ref[s], 0.0)
    local = [jnp.maximum(pb[s], 0) // NROW for s in range(SL)]
    tag = jnp.zeros((SHARE, 128), F32)
    tags = lax.broadcasted_iota(jnp.int32, (SHARE, 128), 1)
    for s in range(SL):
        tag = jnp.where(tags == s, local[s].astype(F32), tag)
    told[...] = tag[0:8]
    c_ref[q] = xv[...]

    pl.semaphore_wait(barrier, 7 + NY - 1 + NZ - 1 + jnp.where(fixed, 0, 1))

    sends = []

    def send(*args):
        copy = rcopy(*args)
        copy.start()
        sends.append(copy)

    piece = xv.at[:, W:OWN]
    mine = xv
    out = rcopy(piece, g_ref.at[half * NCOL + q], ps.at[0], pr.at[0], swap)
    keep = pltpu.make_async_copy(piece, g_ref.at[p], lsem.at[0])
    out_tag = rcopy(told, heard.at[0], ps.at[1], pr.at[1], swap)
    keep_tag = pltpu.make_async_copy(told, heard.at[0], lsem.at[1])

    @pl.when(jnp.logical_not(fixed))
    def _():
        out.start()
        out_tag.start()

    @pl.when(fixed)
    def _():
        keep.start()
        keep_tag.start()

    def ring(t, src_up, src_down):
        if src_up is not None:
            at = zh * NY + (y + NY - t) % NY
            send(src_up, c_ref.at[at], cus.at[t], cur.at[t], up)
        if src_down is not None:
            at = zh * NY + (y + t) % NY
            send(src_down, c_ref.at[at], cds.at[t], cdr.at[t], down)

    def ring_wait(t):
        got = c_ref.at[zh * NY + (y + NY - 1 - t) % NY]
        rcopy(got, got, cus.at[t], cur.at[t], up).wait_recv()
        if t < 3:
            ring(t + 1, got, None)
        if t < 3:
            got = c_ref.at[zh * NY + (y + 1 + t) % NY]
            rcopy(got, got, cds.at[t], cdr.at[t], down).wait_recv()
            if t < 2:
                ring(t + 1, None, got)

    send(mine, c_ref.at[q], chs.at[0], chr_.at[0], far)
    ring(0, mine, mine)

    load_s.wait()
    for s in range(SL):
        for c in range(8):
            blocks = [sv[pl.ds(r * B * 8 + c, B, stride=8), :] for r in range(RC)]
            sub8[s * B : (s + 1) * B, c * B : (c + 1) * B] = pick(blocks, local[s])

    ring_wait(0)
    ring_wait(1)
    other = c_ref.at[(1 - zh) * NY + y]
    rcopy(other, other, chs.at[0], chr_.at[0], far).wait_recv()
    for d in (4, 3, 5, 2, 6, 1, 7):
        send(other, other, cas.at[d - 1], car.at[d - 1], ydev[d])

    @pl.when(jnp.logical_not(fixed))
    def _():
        rcopy(piece, g_ref.at[p], ps.at[0], pr.at[0], swap).wait_recv()
        out_tag.wait_recv()

    @pl.when(fixed)
    def _():
        keep.wait()
        keep_tag.wait()

    def fan(src, dz):
        got = g_ref.at[src]
        for d in (2, 1, 3) if dz == 2 else (1, 3):
            send(got, got, gxs.at[dz * 3 + d - 1], gxr.at[dz * 3 + d - 1], xk[d, 0])
        send(got, got, gks.at[dz * 4], gkr.at[dz * 4], core)

    own = g_ref.at[p]
    for d in (1, 3, 2):
        send(own, own, gzs.at[d - 1], gzr.at[d - 1], lzdev[d])
    fan(p, 0)
    send(heard.at[0], heard.at[1], gxs.at[12], gxr.at[12], xk[2, 0])

    def z_wait(d):
        src = row_id(x, (zl + NZL - d) % NZL, k)
        got = g_ref.at[src]
        rcopy(got, got, gzs.at[d - 1], gzr.at[d - 1], lzdev[d]).wait_recv()
        fan(src, d)

    def x_wait(dz, d):
        src = row_id((x + NX - d) % NX, (zl + NZL - dz) % NZL, k)
        got = g_ref.at[src]
        n = dz * 3 + d - 1
        rcopy(got, got, gxs.at[n], gxr.at[n], xk[d, 0]).wait_recv()
        n = dz * 3 + 1
        if (dz, d) in ((0, 1), (1, 3), (3, 3)):
            send(got, got, gxs.at[n], gxr.at[n], xk[d, 0])
        send(got, got, gks.at[dz * 4 + d], gkr.at[dz * 4 + d], core)

    ring_wait(2)
    z_wait(1)
    z_wait(3)
    x_wait(0, 1)
    x_wait(0, 3)
    z_wait(2)
    x_wait(0, 2)
    x_wait(1, 1)
    x_wait(1, 3)
    x_wait(3, 1)
    x_wait(3, 3)
    x_wait(1, 2)
    x_wait(3, 2)
    x_wait(2, 1)
    x_wait(2, 3)
    x_wait(2, 2)

    rcopy(heard.at[1], heard.at[1], gxs.at[12], gxr.at[12], xk[2, 0]).wait_recv()
    said = [[jnp.max(jnp.where(tags[0:8] == t, heard[h], 0.0)) for t in range(SL)] for h in range(2)]
    for h in range(2):
        for t in range(SL):
            which = jnp.where(half == h, said[0][t], said[1][t])
            for s in range(SL):
                at = slice(s * B, (s + 1) * B)
                n = h * SL + t
                value = sub8[at, h * B : (h + 1) * B]
                for r in range(1, RC):
                    block = sub8[at, (2 * r + h) * B : (2 * r + h + 1) * B]
                    value = jnp.where(which > r - 0.5, block, value)
                sub[at, n * B : (n + 1) * B] = value

    for dz in (0, 1, 3, 2):
        for d in (0, 1, 3, 2):
            src = row_id((x + NX - d) % NX, (zl + NZL - dz) % NZL, 1 - k)
            got = g_ref.at[src]
            rcopy(got, got, gks.at[dz * 4 + d], gkr.at[dz * 4 + d], core).wait_recv()

    def panel(h, at):
        return halves(g_ref[h * NCOL : (h + 1) * NCOL, :, at : at + ROWS].reshape(W, ROWS))

    gp = [panel(h, 0) for h in range(2)]
    gq = [panel(h, ROWS) for h in range(2)]
    for s in range(SL):
        at = slice(s * B, (s + 1) * B)
        left = [halves(sub[at, h * ROWS : (h + 1) * ROWS]) for h in range(2)]
        yv[at, :] = dot3(left[0], gp[0], NT) + dot3(left[1], gp[1], NT)
        zv[at, :] = dot3(left[0], gq[0], NT) + dot3(left[1], gq[1], NT)
    ring_wait(3)
    for d in (1, 7, 2, 6, 3, 5, 4):
        got = c_ref.at[(1 - zh) * NY + (y + NY - d) % NY]
        rcopy(got, got, cas.at[d - 1], car.at[d - 1], ydev[d]).wait_recv()
    topf = c_ref[:, :, 0:W].reshape(W, W)
    top = halves(topf)
    rows = lax.broadcasted_iota(jnp.int32, (B, 1), 0)
    for s in range(SL):
        at = slice(s * B, (s + 1) * B)
        yy = jnp.where(rows < psz[s], -yv[at, :], 0.0)
        zz = jnp.where(rows < csz[s], -(zv[at, :] + dot3(halves(yy), top, NN)), 0.0)
        yv[at, :] = yy
        zv[at, :] = zz
        yz[:, :, s * CB : (s + 1) * CB, 0:W] = yy.reshape(NZH, NY, CB, W)
        yz[:, :, s * CB : (s + 1) * CB, W : 2 * W] = zz.reshape(NZH, NY, CB, W)

    def sum_up(a, t):
        n = a * 4 + t
        dst = ubuf.at[n]
        if t == 0:
            src = yz.at[a, (y + UPS[a]) % NY]
        else:
            src = ubuf.at[n - 1]
            rcopy(src, src, us.at[n - 1], ur.at[n - 1], up).wait_recv()
            ubuf[n - 1] = ubuf[n - 1] + yz[a, (y + UPS[a] - t) % NY]
        send(src, dst, us.at[n], ur.at[n], up)

    def sum_down(a, t):
        n = a * 4 + t
        dst = dbuf.at[n]
        if t == 0:
            src = yz.at[a, (y + NY - DOWNS[a]) % NY]
        else:
            src = dbuf.at[n - 1]
            rcopy(src, src, ds.at[n - 1], dr.at[n - 1], down).wait_recv()
            dbuf[n - 1] = dbuf[n - 1] + yz[a, (y + NY - DOWNS[a] + t) % NY]
        send(src, dst, ds.at[n], dr.at[n], down)

    def sum_step(t):
        for a in range(2):
            if t < UPS[a]:
                sum_up(a, t)
            if t < DOWNS[a]:
                sum_down(a, t)

    sum_step(0)

    def put(m, mat):
        for n in range(2):
            aue[n, m] = mat[:, n * 128 : (n + 1) * 128]
        send(aue.at[1 - k, m], kbuf.at[m], ks.at[m], kr.at[m], core)

    pp = halves(c_ref[:, :, W : W + ROWS].reshape(W, ROWS))
    qp = halves(c_ref[:, :, W + ROWS : OWN].reshape(W, ROWS))
    ysp = halves(yv[...])
    a_mat = dot3(pp, ysp, NN)
    put(0, a_mat)
    uv[...] = dot3(halves(a_mat), top, NN) - dot3(qp, ysp, NN).T
    first = jnp.where(p == 0, 1.0, 0.0)
    mid = pl.ds(pl.multiple_of(q * SHARE, SHARE), SHARE)
    uv[mid, :] = uv[mid, :] - first * dot3(halves(d_ref[...]), top, NN)
    u_mat = uv[...]
    put(1, u_mat)
    e_mat = -dot3(halves(topf.T), halves(u_mat), NN) - dot3(qp, halves(zv[...]), NN)
    put(2, e_mat)

    busy = x < 3
    ahead, behind = xk[1, 0], xk[3, 0]
    nxt, prv = (x + 1) % NX, (x + 3) % NX

    def xcopy(n, m, part, dev):
        return rcopy(acc.at[m, part], xbuf.at[n], xs.at[n], xr.at[n], dev)

    def landed(n, dev):
        rcopy(xbuf.at[n], xbuf.at[n], xs.at[n], xr.at[n], dev).wait_recv()

    def relay_up():
        return xcopy(0, (x + 2) % NX, 1, ahead)

    def relay_down():
        return xcopy(1, (x + 2) % NX, 0, behind)

    def plain_up():
        return xcopy(2, nxt, 0, ahead)

    def plain_down():
        return xcopy(3, prv, 1, behind)

    def total_up():
        return xcopy(4, nxt, 1, ahead)

    def total_down():
        return xcopy(5, prv, 0, behind)

    def merge(m):
        got = kbuf.at[m]
        rcopy(got, got, ks.at[m], kr.at[m], core).wait_recv()
        acc[m] = (aue[k, m] + kbuf[m]).reshape(2, 128, 128)

    opposite = (x + 2) % NX

    @pl.when(opposite < 3)
    def _():
        merge(opposite)
        relay_up().start()
        relay_down().start()

    @pl.when(nxt < 3)
    def _():
        merge(nxt)
        plain_up().start()

    @pl.when(prv < 3)
    def _():
        merge(prv)
        plain_down().start()

    @pl.when(busy)
    def _():
        merge(x)

    sum_step(1)
    sum_step(2)

    @pl.when(nxt < 3)
    def _():
        landed(0, ahead)
        acc[nxt, 1] = acc[nxt, 1] + xbuf[0]
        total_up().start()

    @pl.when(prv < 3)
    def _():
        landed(1, behind)
        acc[prv, 0] = acc[prv, 0] + xbuf[1]
        total_down().start()

    sum_step(3)

    def ycopy(d):
        return rcopy(accx.at[:, (y + d) % NY], ybuf.at[d - 1], ys.at[d - 1], yr.at[d - 1], ydev[d])

    def zcopy(d):
        return rcopy(accy.at[zpos[d] // NZL], zbuf.at[d - 1], zs.at[d - 1], zr.at[d - 1], zdev[d])

    def fcopy(d, f):
        n = d * 2 + f - 1
        return rcopy(auo.at[x, k], auo.at[x, k], fs.at[n], fr.at[n], xk[d, f])

    @pl.when(busy)
    def _():
        for n in range(2, 6):
            landed(n, ahead if n % 2 == 0 else behind)
        low = acc[x, 0] + (xbuf[2] + xbuf[5])
        high = acc[x, 1] + (xbuf[3] + xbuf[4])
        accx[0] = low.reshape(NY, SHARE, 128)
        accx[1] = high.reshape(NY, SHARE, 128)
        for d in (4, 3, 5, 2, 6, 1, 7):
            ycopy(d).start()

    for a in range(2):
        n = a * 4 + UPS[a] - 1
        got = ubuf.at[n]
        rcopy(got, got, us.at[n], ur.at[n], up).wait_recv()
        n2 = a * 4 + DOWNS[a] - 1
        got = dbuf.at[n2]
        rcopy(got, got, ds.at[n2], dr.at[n2], down).wait_recv()
        yzacc[a] = yz[a, y] + (ubuf[n] + dbuf[n2])
    send(yzacc.at[1 - zh], hbuf, hs.at[0], hr.at[0], far)

    hop = rcopy(hbuf, hbuf, hs.at[0], hr.at[0], far)
    @pl.when(busy)
    def _():
        for d in range(1, NY):
            ycopy(d).wait_recv()
        total = accx[:, y]
        for d in range(NY - 1):
            total = total + ybuf[d]
        accy[...] = total
        for d in (4, 3, 5, 2, 6, 1, 7):
            zcopy(d).start()

    hop.wait_recv()
    yzo[...] = yzacc[zh] + hbuf[...]

    @pl.when(busy)
    def _():
        for d in range(1, NZ):
            zcopy(d).wait_recv()
        total = accy[zh]
        for d in range(NZ - 1):
            total = total + zbuf[d]
        auo[x, k] = total
        for d, f in xk:
            fcopy(d, f).start()

    for d, f in xk:
        m = (x + NX - d) % NX
        n = d * 2 + f - 1

        @pl.when(m < 3)
        def _():
            got = auo.at[m, k if f == 0 else 1 - k]
            rcopy(got, got, fs.at[n], fr.at[n], xk[d, f]).wait_recv()

    @pl.when(jnp.logical_not(fixed))
    def _():
        out.wait_send()
        out_tag.wait_send()

    for copy in sends:
        copy.wait_send()

    @pl.when((x + 2) % NX < 3)
    def _():
        relay_up().wait_send()
        relay_down().wait_send()

    @pl.when(nxt < 3)
    def _():
        plain_up().wait_send()
        total_up().wait_send()

    @pl.when(prv < 3)
    def _():
        plain_down().wait_send()
        total_down().wait_send()

    @pl.when(busy)
    def _():
        for d in range(1, NY):
            ycopy(d).wait_send()
        for d in range(1, NZ):
            zcopy(d).wait_send()
        for d, f in xk:
            fcopy(d, f).wait_send()


def step(*operands):
    vmem = pl.BlockSpec(memory_space=pltpu.VMEM)
    dma = pltpu.SemaphoreType.DMA
    rows = SL * CB
    buffers = [
        (SL, SHARE, B),
        (SL, SHARE, B),
        (SHARE, W),
        (RC * B * 8, B),
        (ROWS, 8 * B),
        (ROWS, 2 * ROWS),
        (SHARE, OWN),
        (8, 128),
        (2, 8, 128),
        (NROW, SHARE, PATCH),
        (NCOL, SHARE, OWN),
        (ROWS, W),
        (ROWS, W),
        (W, W),
        (NZH, NY, rows, 2 * W),
        (2, 3, W, 128),
        (3, W, 128),
        (3, 2, 128, 128),
        (6, 128, 128),
        (NZH, NY, SHARE, 128),
        (NY - 1, NZH, SHARE, 128),
        (NZH, SHARE, 128),
        (NZ - 1, SHARE, 128),
        (8, rows, 2 * W),
        (8, rows, 2 * W),
        (NZH, rows, 2 * W),
        (rows, 2 * W),
    ]
    sems = [1, 7, 2, 2, 2, 3, 3, 13, 13, 16, 16, 1, 1, 4, 4, 3, 3, 7, 7]
    sems += [3, 3, 6, 6, 7, 7, 7, 7, 7, 7, 8, 8, 8, 8, 1, 1]
    return pl.pallas_call(
        step_kernel,
        out_shape=(
            jax.ShapeDtypeStruct((rows, 2 * W), F32),
            jax.ShapeDtypeStruct((3, 2, SHARE, 128), F32),
        ),
        in_specs=[pl.BlockSpec(memory_space=pl.ANY)] * 8,
        out_specs=(vmem, vmem),
        scratch_shapes=[pltpu.SMEM((SL,), jnp.int32)] * 3
        + [pltpu.VMEM(b, F32) for b in buffers]
        + [dma((n,)) for n in sems],
        compiler_params=pltpu.CompilerParams(collective_id=0, has_side_effects=True),
        name="step",
    )(*operands)


def place_kernel(pb, yz_ref, mats_ref, d_ref, cd_ref, prow, pd, crow, cu, cdiag):
    p = lax.axis_index("row")
    for r in range(RC):
        ya = jnp.zeros((CB, W), F32)
        za = jnp.zeros((CB, W), F32)
        for s in range(SL):
            here = pb[s] == r * NROW + p
            ya = jnp.where(here, yz_ref[s * CB : (s + 1) * CB, 0:W], ya)
            za = jnp.where(here, yz_ref[s * CB : (s + 1) * CB, W:], za)
        prow[r] = ya
        crow[r] = za
    for n in range(2):
        at = slice(n * 128, (n + 1) * 128)
        pd[:, at] = d_ref[:, at] - mats_ref[0, n]
        cu[:, at] = mats_ref[1, n]
        cdiag[:, at] = cd_ref[:, at] + mats_ref[2, n]


def lay(*operands):
    vmem = pl.BlockSpec(memory_space=pltpu.VMEM)
    smem = pl.BlockSpec(memory_space=pltpu.SMEM)
    share = jax.ShapeDtypeStruct((SHARE, W), F32)
    rows = jax.ShapeDtypeStruct((RC, CB, W), F32)
    return pl.pallas_call(
        place_kernel,
        out_shape=(rows, share, rows, share, share),
        in_specs=[smem] + [vmem] * 4,
        out_specs=(vmem,) * 5,
        name="lay",
    )(*operands)


def body(
    cached_inverse,
    parent_panel,
    parent_blocks,
    parent_sizes,
    parent_diagonal,
    child_panel,
    child_top,
    child_blocks,
    child_sizes,
    child_diagonal,
):
    rows, mats = step(
        parent_blocks,
        parent_sizes,
        child_sizes,
        cached_inverse.reshape(RC * B * 8, B),
        jnp.transpose(parent_panel, (1, 0, 2)),
        jnp.transpose(child_panel, (1, 0, 2)),
        child_top,
        parent_diagonal,
    )
    prow, pd, crow, cu, cdiag = lay(parent_blocks, rows, mats, parent_diagonal, child_diagonal)
    return (prow[:, None], pd, crow[:, None], cu, cdiag)


def solution(mesh):
    in_specs = (
        P(None, "row", None, None, "col", None),
        P("col", "row", None),
        P("row"),
        P("row"),
        P("col", None),
        P("col", "row", None),
        P("col", None),
        P("row"),
        P("row"),
        P("col", None),
    )
    out_specs = (
        P(None, "row", "col", None),
        P("col", None),
        P(None, "row", "col", None),
        P("col", None),
        P("col", None),
    )
    return jax.shard_map(body, mesh=mesh, in_specs=in_specs, out_specs=out_specs, check_vma=False)
```

```python
import jax
import jax.numpy as jnp
from jax import lax
from jax.experimental import pallas as pl
from jax.experimental.pallas import tpu as pltpu
from jax.sharding import PartitionSpec as P

MESH = pl.DeviceIdType.MESH
F32 = jnp.float32
BF16 = jnp.bfloat16

NX, NZL, NZH, NY, NK = 4, 4, 2, 8, 2
NZ = NZL * NZH
NROW, NCOL = NX * NZL * NK, NZH * NY
W, B, SL, RC = 256, 128, 3, 4
SHARE = W // NCOL
ROWS = SL * B
CB = B // NCOL
PATCH = 2 * ROWS
OWN = W + PATCH
RING_UPS = (4, 3, 3)
RING_DOWNS = (3, 4, 4)
UPS = (4, 3)
DOWNS = (3, 4)


def place():
    p = lax.axis_index("row")
    q = lax.axis_index("col")
    x = p // (NZL * NK)
    zl = (p // NK) % NZL
    k = p % NK
    return p, q, x, zl, k, q // NY, q % NY


def row_id(x, zl, k):
    return (x * NZL + zl) * NK + k


def rcopy(src, dst, send, recv, target):
    return pltpu.make_async_remote_copy(
        src_ref=src,
        dst_ref=dst,
        send_sem=send,
        recv_sem=recv,
        device_id=target,
        device_id_type=MESH,
    )


def halves(a):
    hi = a.astype(BF16)
    lo = (a - hi.astype(F32)).astype(BF16)
    return hi, lo


def dot3(a, b, dims):
    def one(u, v):
        return lax.dot_general(u, v, (dims, ((), ())), preferred_element_type=F32)

    return one(a[0], b[0]) + (one(a[0], b[1]) + one(a[1], b[0]))


NN = ((1,), (0,))
NT = ((1,), (1,))


def pick(values, which, first=0):
    out = values[0]
    for n in range(1, len(values)):
        out = jnp.where(which == n, values[n], out)
    return out


def step_kernel(
    pb_hbm, psz_hbm, csz_hbm, s_hbm, pp_hbm, cp_hbm, top_hbm, d_hbm,
    yzo, auo,
    pb, psz, csz, pp_ref, cp_ref, d_ref, sv, sub8, sub, xv, told, heard, g_ref, c_ref, yv, zv, uv, yz, aue,
    kbuf, acc, xbuf, accx, ybuf, accy, zbuf, ubuf, dbuf, yzacc, hbuf,
    ssem, isem, ps, pr, lsem, gzs, gzr, gxs, gxr, gks, gkr, chs, chr_, cus, cur, cds, cdr,
    ks, kr, xs, xr, ys, yr, zs, zr, fs, fr, us, ur, ds, dr, hs, hr,
):
    p, q, x, zl, k, zh, y = place()
    z = zh * NZL + zl
    half, cls = p // NCOL, p % NCOL
    fixed = q == cls
    swap = (half * NCOL + q, cls)
    xk = {}
    for d in range(NX):
        for f in range(2):
            if d or f:
                xk[d, f] = (row_id((x + d) % NX, zl, k if f == 0 else 1 - k), q)
    core = xk[0, 1]
    lzdev = [None] + [(row_id(x, (zl + d) % NZL, k), q) for d in range(1, NZL)]
    ydev = [None] + [(p, zh * NY + (y + d) % NY) for d in range(1, NY)]
    up, down = ydev[1], ydev[NY - 1]
    zpos = [(z + d) % NZ for d in range(NZ)]
    zdev = [None] + [(row_id(x, zpos[d] % NZL, k), (zpos[d] // NZL) * NY + y) for d in range(1, NZ)]
    far = zdev[NZL]

    barrier = pltpu.get_barrier_semaphore()

    @pl.when(jnp.logical_not(fixed))
    def _():
        pl.semaphore_signal(barrier, inc=1, device_id=swap, device_id_type=MESH)

    for dev in zdev[1:] + ydev[1:] + list(xk.values()):
        pl.semaphore_signal(barrier, inc=1, device_id=dev, device_id_type=MESH)

    loads = [
        pltpu.make_async_copy(src, dst, isem.at[n])
        for n, (src, dst) in enumerate((
            (psz_hbm, psz),
            (csz_hbm, csz),
            (pb_hbm, pb),
            (pp_hbm, pp_ref),
            (cp_hbm, cp_ref),
            (top_hbm, xv.at[:, 0:W]),
            (d_hbm, d_ref),
        ))
    ]
    for load in loads:
        load.start()
    load_s = pltpu.make_async_copy(s_hbm, sv, ssem.at[0])
    load_s.start()
    for load in loads:
        load.wait()

    lane = lax.broadcasted_iota(jnp.int32, (SHARE, B), 1)
    for s in range(SL):
        at = W + s * B
        xv[:, at : at + B] = jnp.where(lane < psz[s], pp_ref[s], 0.0)
        at += ROWS
        xv[:, at : at + B] = jnp.where(lane < csz[s], cp_ref[s], 0.0)
    local = [jnp.maximum(pb[s], 0) // NROW for s in range(SL)]
    tag = jnp.zeros((SHARE, 128), F32)
    tags = lax.broadcasted_iota(jnp.int32, (SHARE, 128), 1)
    for s in range(SL):
        tag = jnp.where(tags == s, local[s].astype(F32), tag)
    told[...] = tag[0:8]
    c_ref[q] = xv[...]

    pl.semaphore_wait(barrier, 7 + NY - 1 + NZ - 1 + jnp.where(fixed, 0, 1))

    sends = []

    def send(*args):
        copy = rcopy(*args)
        copy.start()
        sends.append(copy)

    piece = xv.at[:, W:OWN]
    mine = xv
    out = rcopy(piece, g_ref.at[half * NCOL + q], ps.at[0], pr.at[0], swap)
    keep = pltpu.make_async_copy(piece, g_ref.at[p], lsem.at[0])
    out_tag = rcopy(told, heard.at[0], ps.at[1], pr.at[1], swap)
    keep_tag = pltpu.make_async_copy(told, heard.at[0], lsem.at[1])

    @pl.when(jnp.logical_not(fixed))
    def _():
        out.start()
        out_tag.start()

    @pl.when(fixed)
    def _():
        keep.start()
        keep_tag.start()

    def part(a, row):
        return c_ref.at[row] if a == 0 else c_ref.at[row, :, pl.ds((a - 1) * (OWN // 2), OWN // 2)]

    def ring_row(a, at):
        return (zh if a == 0 else 1 - zh) * NY + (y + NY + at) % NY

    def ring(a, t, src_up, src_down):
        n = a * 4 + t
        if src_up is not None:
            send(src_up, part(a, ring_row(a, -t)), cus.at[n], cur.at[n], up)
        if src_down is not None:
            send(src_down, part(a, ring_row(a, t)), cds.at[n], cdr.at[n], down)

    def ring_wait(a, t):
        n = a * 4 + t
        if t < RING_UPS[a]:
            got = part(a, ring_row(a, -1 - t))
            rcopy(got, got, cus.at[n], cur.at[n], up).wait_recv()
            if t + 1 < RING_UPS[a]:
                ring(a, t + 1, got, None)
        if t < RING_DOWNS[a]:
            got = part(a, ring_row(a, 1 + t))
            rcopy(got, got, cds.at[n], cdr.at[n], down).wait_recv()
            if t + 1 < RING_DOWNS[a]:
                ring(a, t + 1, None, got)

    for a in (1, 2):
        side = xv.at[:, pl.ds((a - 1) * (OWN // 2), OWN // 2)]
        send(side, part(a, q), chs.at[a - 1], chr_.at[a - 1], far)
    ring(0, 0, mine, mine)

    load_s.wait()
    for s in range(SL):
        for c in range(8):
            blocks = [sv[pl.ds(r * B * 8 + c, B, stride=8), :] for r in range(RC)]
            sub8[s * B : (s + 1) * B, c * B : (c + 1) * B] = pick(blocks, local[s])

    ring_wait(0, 0)
    ring_wait(0, 1)
    for a in (1, 2):
        other = part(a, (1 - zh) * NY + y)
        rcopy(other, other, chs.at[a - 1], chr_.at[a - 1], far).wait_recv()
        ring(a, 0, other, other)

    @pl.when(jnp.logical_not(fixed))
    def _():
        rcopy(piece, g_ref.at[p], ps.at[0], pr.at[0], swap).wait_recv()
        out_tag.wait_recv()

    @pl.when(fixed)
    def _():
        keep.wait()
        keep_tag.wait()

    def fan(src, dz):
        got = g_ref.at[src]
        for d in (2, 1, 3) if dz == 2 else (1, 3):
            send(got, got, gxs.at[dz * 3 + d - 1], gxr.at[dz * 3 + d - 1], xk[d, 0])
        send(got, got, gks.at[dz * 4], gkr.at[dz * 4], core)

    own = g_ref.at[p]
    for d in (1, 3, 2):
        send(own, own, gzs.at[d - 1], gzr.at[d - 1], lzdev[d])
    fan(p, 0)
    send(heard.at[0], heard.at[1], gxs.at[12], gxr.at[12], xk[2, 0])

    def z_wait(d):
        src = row_id(x, (zl + NZL - d) % NZL, k)
        got = g_ref.at[src]
        rcopy(got, got, gzs.at[d - 1], gzr.at[d - 1], lzdev[d]).wait_recv()
        fan(src, d)

    def x_wait(dz, d):
        src = row_id((x + NX - d) % NX, (zl + NZL - dz) % NZL, k)
        got = g_ref.at[src]
        n = dz * 3 + d - 1
        rcopy(got, got, gxs.at[n], gxr.at[n], xk[d, 0]).wait_recv()
        n = dz * 3 + 1
        if (dz, d) in ((0, 1), (1, 3), (3, 3)):
            send(got, got, gxs.at[n], gxr.at[n], xk[d, 0])
        send(got, got, gks.at[dz * 4 + d], gkr.at[dz * 4 + d], core)

    ring_wait(0, 2)
    z_wait(1)
    z_wait(3)
    x_wait(0, 1)
    x_wait(0, 3)
    ring_wait(1, 0)
    ring_wait(2, 0)
    z_wait(2)
    x_wait(0, 2)
    ring_wait(0, 3)
    x_wait(1, 1)
    x_wait(1, 3)
    ring_wait(1, 1)
    ring_wait(2, 1)
    x_wait(3, 1)
    x_wait(3, 3)
    x_wait(1, 2)
    x_wait(3, 2)
    x_wait(2, 1)
    x_wait(2, 3)
    ring_wait(1, 2)
    ring_wait(2, 2)
    x_wait(2, 2)

    rcopy(heard.at[1], heard.at[1], gxs.at[12], gxr.at[12], xk[2, 0]).wait_recv()
    said = [[jnp.max(jnp.where(tags[0:8] == t, heard[h], 0.0)) for t in range(SL)] for h in range(2)]
    for h in range(2):
        for t in range(SL):
            which = jnp.where(half == h, said[0][t], said[1][t])
            for s in range(SL):
                at = slice(s * B, (s + 1) * B)
                n = h * SL + t
                value = sub8[at, h * B : (h + 1) * B]
                for r in range(1, RC):
                    block = sub8[at, (2 * r + h) * B : (2 * r + h + 1) * B]
                    value = jnp.where(which > r - 0.5, block, value)
                sub[at, n * B : (n + 1) * B] = value

    for dz in (0, 1, 3, 2):
        for d in (0, 1, 3, 2):
            src = row_id((x + NX - d) % NX, (zl + NZL - dz) % NZL, 1 - k)
            got = g_ref.at[src]
            rcopy(got, got, gks.at[dz * 4 + d], gkr.at[dz * 4 + d], core).wait_recv()

    def panel(h, at):
        return halves(g_ref[h * NCOL : (h + 1) * NCOL, :, at : at + ROWS].reshape(W, ROWS))

    gp = [panel(h, 0) for h in range(2)]
    gq = [panel(h, ROWS) for h in range(2)]
    for s in range(SL):
        at = slice(s * B, (s + 1) * B)
        left = [halves(sub[at, h * ROWS : (h + 1) * ROWS]) for h in range(2)]
        yv[at, :] = dot3(left[0], gp[0], NT) + dot3(left[1], gp[1], NT)
        zv[at, :] = dot3(left[0], gq[0], NT) + dot3(left[1], gq[1], NT)
    ring_wait(1, 3)
    ring_wait(2, 3)
    topf = c_ref[:, :, 0:W].reshape(W, W)
    top = halves(topf)
    rows = lax.broadcasted_iota(jnp.int32, (B, 1), 0)
    for s in range(SL):
        at = slice(s * B, (s + 1) * B)
        yy = jnp.where(rows < psz[s], -yv[at, :], 0.0)
        zz = jnp.where(rows < csz[s], -(zv[at, :] + dot3(halves(yy), top, NN)), 0.0)
        yv[at, :] = yy
        zv[at, :] = zz
        yz[:, :, s * CB : (s + 1) * CB, 0:W] = yy.reshape(NZH, NY, CB, W)
        yz[:, :, s * CB : (s + 1) * CB, W : 2 * W] = zz.reshape(NZH, NY, CB, W)

    def sum_up(a, t):
        n = a * 4 + t
        dst = ubuf.at[n]
        if t == 0:
            src = yz.at[a, (y + UPS[a]) % NY]
        else:
            src = ubuf.at[n - 1]
            rcopy(src, src, us.at[n - 1], ur.at[n - 1], up).wait_recv()
            ubuf[n - 1] = ubuf[n - 1] + yz[a, (y + UPS[a] - t) % NY]
        send(src, dst, us.at[n], ur.at[n], up)

    def sum_down(a, t):
        n = a * 4 + t
        dst = dbuf.at[n]
        if t == 0:
            src = yz.at[a, (y + NY - DOWNS[a]) % NY]
        else:
            src = dbuf.at[n - 1]
            rcopy(src, src, ds.at[n - 1], dr.at[n - 1], down).wait_recv()
            dbuf[n - 1] = dbuf[n - 1] + yz[a, (y + NY - DOWNS[a] + t) % NY]
        send(src, dst, ds.at[n], dr.at[n], down)

    def sum_step(t):
        for a in range(2):
            if t < UPS[a]:
                sum_up(a, t)
            if t < DOWNS[a]:
                sum_down(a, t)

    sum_step(0)

    def put(m, mat):
        for n in range(2):
            aue[n, m] = mat[:, n * 128 : (n + 1) * 128]
        send(aue.at[1 - k, m], kbuf.at[m], ks.at[m], kr.at[m], core)

    pp = halves(c_ref[:, :, W : W + ROWS].reshape(W, ROWS))
    qp = halves(c_ref[:, :, W + ROWS : OWN].reshape(W, ROWS))
    ysp = halves(yv[...])
    a_mat = dot3(pp, ysp, NN)
    put(0, a_mat)
    uv[...] = dot3(halves(a_mat), top, NN) - dot3(qp, ysp, NN).T
    first = jnp.where(p == 0, 1.0, 0.0)
    mid = pl.ds(pl.multiple_of(q * SHARE, SHARE), SHARE)
    uv[mid, :] = uv[mid, :] - first * dot3(halves(d_ref[...]), top, NN)
    u_mat = uv[...]
    put(1, u_mat)
    e_mat = -dot3(halves(topf.T), halves(u_mat), NN) - dot3(qp, halves(zv[...]), NN)
    put(2, e_mat)

    busy = x < 3
    ahead, behind = xk[1, 0], xk[3, 0]
    nxt, prv = (x + 1) % NX, (x + 3) % NX

    def xcopy(n, m, part, dev):
        return rcopy(acc.at[m, part], xbuf.at[n], xs.at[n], xr.at[n], dev)

    def landed(n, dev):
        rcopy(xbuf.at[n], xbuf.at[n], xs.at[n], xr.at[n], dev).wait_recv()

    def relay_up():
        return xcopy(0, (x + 2) % NX, 1, ahead)

    def relay_down():
        return xcopy(1, (x + 2) % NX, 0, behind)

    def plain_up():
        return xcopy(2, nxt, 0, ahead)

    def plain_down():
        return xcopy(3, prv, 1, behind)

    def total_up():
        return xcopy(4, nxt, 1, ahead)

    def total_down():
        return xcopy(5, prv, 0, behind)

    def merge(m):
        got = kbuf.at[m]
        rcopy(got, got, ks.at[m], kr.at[m], core).wait_recv()
        acc[m] = (aue[k, m] + kbuf[m]).reshape(2, 128, 128)

    opposite = (x + 2) % NX

    @pl.when(opposite < 3)
    def _():
        merge(opposite)
        relay_up().start()
        relay_down().start()

    @pl.when(nxt < 3)
    def _():
        merge(nxt)
        plain_up().start()

    @pl.when(prv < 3)
    def _():
        merge(prv)
        plain_down().start()

    @pl.when(busy)
    def _():
        merge(x)

    sum_step(1)
    sum_step(2)

    @pl.when(nxt < 3)
    def _():
        landed(0, ahead)
        acc[nxt, 1] = acc[nxt, 1] + xbuf[0]
        total_up().start()

    @pl.when(prv < 3)
    def _():
        landed(1, behind)
        acc[prv, 0] = acc[prv, 0] + xbuf[1]
        total_down().start()

    sum_step(3)

    def ycopy(d):
        return rcopy(accx.at[:, (y + d) % NY], ybuf.at[d - 1], ys.at[d - 1], yr.at[d - 1], ydev[d])

    def zcopy(d):
        return rcopy(accy.at[zpos[d] // NZL], zbuf.at[d - 1], zs.at[d - 1], zr.at[d - 1], zdev[d])

    def fcopy(d, f):
        n = d * 2 + f - 1
        return rcopy(auo.at[x, k], auo.at[x, k], fs.at[n], fr.at[n], xk[d, f])

    @pl.when(busy)
    def _():
        for n in range(2, 6):
            landed(n, ahead if n % 2 == 0 else behind)
        low = acc[x, 0] + (xbuf[2] + xbuf[5])
        high = acc[x, 1] + (xbuf[3] + xbuf[4])
        accx[0] = low.reshape(NY, SHARE, 128)
        accx[1] = high.reshape(NY, SHARE, 128)
        for d in (4, 3, 5, 2, 6, 1, 7):
            ycopy(d).start()

    for a in range(2):
        n = a * 4 + UPS[a] - 1
        got = ubuf.at[n]
        rcopy(got, got, us.at[n], ur.at[n], up).wait_recv()
        n2 = a * 4 + DOWNS[a] - 1
        got = dbuf.at[n2]
        rcopy(got, got, ds.at[n2], dr.at[n2], down).wait_recv()
        yzacc[a] = yz[a, y] + (ubuf[n] + dbuf[n2])
    send(yzacc.at[1 - zh], hbuf, hs.at[0], hr.at[0], far)

    hop = rcopy(hbuf, hbuf, hs.at[0], hr.at[0], far)
    @pl.when(busy)
    def _():
        for d in range(1, NY):
            ycopy(d).wait_recv()
        total = accx[:, y]
        for d in range(NY - 1):
            total = total + ybuf[d]
        accy[...] = total
        for d in (4, 3, 5, 2, 6, 1, 7):
            zcopy(d).start()

    hop.wait_recv()
    yzo[...] = yzacc[zh] + hbuf[...]

    @pl.when(busy)
    def _():
        for d in range(1, NZ):
            zcopy(d).wait_recv()
        total = accy[zh]
        for d in range(NZ - 1):
            total = total + zbuf[d]
        auo[x, k] = total
        for d, f in xk:
            fcopy(d, f).start()

    for d, f in xk:
        m = (x + NX - d) % NX
        n = d * 2 + f - 1

        @pl.when(m < 3)
        def _():
            got = auo.at[m, k if f == 0 else 1 - k]
            rcopy(got, got, fs.at[n], fr.at[n], xk[d, f]).wait_recv()

    @pl.when(jnp.logical_not(fixed))
    def _():
        out.wait_send()
        out_tag.wait_send()

    for copy in sends:
        copy.wait_send()

    @pl.when((x + 2) % NX < 3)
    def _():
        relay_up().wait_send()
        relay_down().wait_send()

    @pl.when(nxt < 3)
    def _():
        plain_up().wait_send()
        total_up().wait_send()

    @pl.when(prv < 3)
    def _():
        plain_down().wait_send()
        total_down().wait_send()

    @pl.when(busy)
    def _():
        for d in range(1, NY):
            ycopy(d).wait_send()
        for d in range(1, NZ):
            zcopy(d).wait_send()
        for d, f in xk:
            fcopy(d, f).wait_send()


def step(*operands):
    vmem = pl.BlockSpec(memory_space=pltpu.VMEM)
    dma = pltpu.SemaphoreType.DMA
    rows = SL * CB
    buffers = [
        (SL, SHARE, B),
        (SL, SHARE, B),
        (SHARE, W),
        (RC * B * 8, B),
        (ROWS, 8 * B),
        (ROWS, 2 * ROWS),
        (SHARE, OWN),
        (8, 128),
        (2, 8, 128),
        (NROW, SHARE, PATCH),
        (NCOL, SHARE, OWN),
        (ROWS, W),
        (ROWS, W),
        (W, W),
        (NZH, NY, rows, 2 * W),
        (2, 3, W, 128),
        (3, W, 128),
        (3, 2, 128, 128),
        (6, 128, 128),
        (NZH, NY, SHARE, 128),
        (NY - 1, NZH, SHARE, 128),
        (NZH, SHARE, 128),
        (NZ - 1, SHARE, 128),
        (8, rows, 2 * W),
        (8, rows, 2 * W),
        (NZH, rows, 2 * W),
        (rows, 2 * W),
    ]
    sems = [1, 7, 2, 2, 2, 3, 3, 13, 13, 16, 16, 2, 2, 12, 12, 12, 12]
    sems += [3, 3, 6, 6, 7, 7, 7, 7, 7, 7, 8, 8, 8, 8, 1, 1]
    return pl.pallas_call(
        step_kernel,
        out_shape=(
            jax.ShapeDtypeStruct((rows, 2 * W), F32),
            jax.ShapeDtypeStruct((3, 2, SHARE, 128), F32),
        ),
        in_specs=[pl.BlockSpec(memory_space=pl.ANY)] * 8,
        out_specs=(vmem, vmem),
        scratch_shapes=[pltpu.SMEM((SL,), jnp.int32)] * 3
        + [pltpu.VMEM(b, F32) for b in buffers]
        + [dma((n,)) for n in sems],
        compiler_params=pltpu.CompilerParams(collective_id=0, has_side_effects=True),
        name="step",
    )(*operands)


def place_kernel(pb, yz_ref, mats_ref, d_ref, cd_ref, prow, pd, crow, cu, cdiag):
    p = lax.axis_index("row")
    for r in range(RC):
        ya = jnp.zeros((CB, W), F32)
        za = jnp.zeros((CB, W), F32)
        for s in range(SL):
            here = pb[s] == r * NROW + p
            ya = jnp.where(here, yz_ref[s * CB : (s + 1) * CB, 0:W], ya)
            za = jnp.where(here, yz_ref[s * CB : (s + 1) * CB, W:], za)
        prow[r] = ya
        crow[r] = za
    for n in range(2):
        at = slice(n * 128, (n + 1) * 128)
        pd[:, at] = d_ref[:, at] - mats_ref[0, n]
        cu[:, at] = mats_ref[1, n]
        cdiag[:, at] = cd_ref[:, at] + mats_ref[2, n]


def lay(*operands):
    vmem = pl.BlockSpec(memory_space=pltpu.VMEM)
    smem = pl.BlockSpec(memory_space=pltpu.SMEM)
    share = jax.ShapeDtypeStruct((SHARE, W), F32)
    rows = jax.ShapeDtypeStruct((RC, CB, W), F32)
    return pl.pallas_call(
        place_kernel,
        out_shape=(rows, share, rows, share, share),
        in_specs=[smem] + [vmem] * 4,
        out_specs=(vmem,) * 5,
        name="lay",
    )(*operands)


def body(
    cached_inverse,
    parent_panel,
    parent_blocks,
    parent_sizes,
    parent_diagonal,
    child_panel,
    child_top,
    child_blocks,
    child_sizes,
    child_diagonal,
):
    rows, mats = step(
        parent_blocks,
        parent_sizes,
        child_sizes,
        cached_inverse.reshape(RC * B * 8, B),
        jnp.transpose(parent_panel, (1, 0, 2)),
        jnp.transpose(child_panel, (1, 0, 2)),
        child_top,
        parent_diagonal,
    )
    prow, pd, crow, cu, cdiag = lay(parent_blocks, rows, mats, parent_diagonal, child_diagonal)
    return (prow[:, None], pd, crow[:, None], cu, cdiag)


def solution(mesh):
    in_specs = (
        P(None, "row", None, None, "col", None),
        P("col", "row", None),
        P("row"),
        P("row"),
        P("col", None),
        P("col", "row", None),
        P("col", None),
        P("row"),
        P("row"),
        P("col", None),
    )
    out_specs = (
        P(None, "row", "col", None),
        P("col", None),
        P(None, "row", "col", None),
        P("col", None),
        P("col", None),
    )
    return jax.shard_map(body, mesh=mesh, in_specs=in_specs, out_specs=out_specs, check_vma=False)
```

```python
import jax
import jax.numpy as jnp
from jax import lax
from jax.experimental import pallas as pl
from jax.experimental.pallas import tpu as pltpu
from jax.sharding import PartitionSpec as P

MESH = pl.DeviceIdType.MESH
F32 = jnp.float32
BF16 = jnp.bfloat16

NX, NZL, NZH, NY, NK = 4, 4, 2, 8, 2
NZ = NZL * NZH
NROW, NCOL = NX * NZL * NK, NZH * NY
W, B, SL, RC = 256, 128, 3, 4
SHARE = W // NCOL
ROWS = SL * B
CB = B // NCOL
PATCH = 2 * ROWS
OWN = W + PATCH
UPS = (4, 3)
DOWNS = (3, 4)


def place():
    p = lax.axis_index("row")
    q = lax.axis_index("col")
    x = p // (NZL * NK)
    zl = (p // NK) % NZL
    k = p % NK
    return p, q, x, zl, k, q // NY, q % NY


def row_id(x, zl, k):
    return (x * NZL + zl) * NK + k


def rcopy(src, dst, send, recv, target):
    return pltpu.make_async_remote_copy(
        src_ref=src,
        dst_ref=dst,
        send_sem=send,
        recv_sem=recv,
        device_id=target,
        device_id_type=MESH,
    )


def halves(a):
    hi = a.astype(BF16)
    lo = (a - hi.astype(F32)).astype(BF16)
    return hi, lo


def dot3(a, b, dims):
    def one(u, v):
        return lax.dot_general(u, v, (dims, ((), ())), preferred_element_type=F32)

    return one(a[0], b[0]) + (one(a[0], b[1]) + one(a[1], b[0]))


NN = ((1,), (0,))
NT = ((1,), (1,))


def pick(values, which, first=0):
    out = values[0]
    for n in range(1, len(values)):
        out = jnp.where(which == n, values[n], out)
    return out


def step_kernel(
    pb_hbm, psz_hbm, csz_hbm, s_hbm, pp_hbm, cp_hbm, top_hbm, d_hbm,
    yzo, auo,
    pb, psz, csz, pp_ref, cp_ref, d_ref, sv, sub8, sub, xv, told, heard, g_ref, c_ref, yv, zv, uv, yz, aue,
    kbuf, acc, xbuf, accx, ybuf, accy, zbuf, ubuf, dbuf, yzacc, hbuf,
    ssem, isem, ps, pr, lsem, gzs, gzr, gxs, gxr, gks, gkr, chs, chr_, cus, cur, cds, cdr,
    ks, kr, xs, xr, ys, yr, zs, zr, fs, fr, us, ur, ds, dr, hs, hr,
):
    p, q, x, zl, k, zh, y = place()
    z = zh * NZL + zl
    half, cls = p // NCOL, p % NCOL
    fixed = q == cls
    swap = (half * NCOL + q, cls)
    xk = {}
    for d in range(NX):
        for f in range(2):
            if d or f:
                xk[d, f] = (row_id((x + d) % NX, zl, k if f == 0 else 1 - k), q)
    core = xk[0, 1]
    lzdev = [None] + [(row_id(x, (zl + d) % NZL, k), q) for d in range(1, NZL)]
    ydev = [None] + [(p, zh * NY + (y + d) % NY) for d in range(1, NY)]
    up, down = ydev[1], ydev[NY - 1]
    zpos = [(z + d) % NZ for d in range(NZ)]
    zdev = [None] + [(row_id(x, zpos[d] % NZL, k), (zpos[d] // NZL) * NY + y) for d in range(1, NZ)]
    far = zdev[NZL]

    barrier = pltpu.get_barrier_semaphore()

    @pl.when(jnp.logical_not(fixed))
    def _():
        pl.semaphore_signal(barrier, inc=1, device_id=swap, device_id_type=MESH)

    for dev in zdev[1:] + ydev[1:] + list(xk.values()):
        pl.semaphore_signal(barrier, inc=1, device_id=dev, device_id_type=MESH)

    loads = [
        pltpu.make_async_copy(src, dst, isem.at[n])
        for n, (src, dst) in enumerate((
            (psz_hbm, psz),
            (csz_hbm, csz),
            (pb_hbm, pb),
            (pp_hbm, pp_ref),
            (cp_hbm, cp_ref),
            (top_hbm, xv.at[:, 0:W]),
            (d_hbm, d_ref),
        ))
    ]
    for load in loads:
        load.start()
    load_s = pltpu.make_async_copy(s_hbm, sv, ssem.at[0])
    load_s.start()
    for load in loads:
        load.wait()

    lane = lax.broadcasted_iota(jnp.int32, (SHARE, B), 1)
    for s in range(SL):
        at = W + s * B
        xv[:, at : at + B] = jnp.where(lane < psz[s], pp_ref[s], 0.0)
        at += ROWS
        xv[:, at : at + B] = jnp.where(lane < csz[s], cp_ref[s], 0.0)
    local = [jnp.maximum(pb[s], 0) // NROW for s in range(SL)]
    tag = jnp.zeros((SHARE, 128), F32)
    tags = lax.broadcasted_iota(jnp.int32, (SHARE, 128), 1)
    for s in range(SL):
        tag = jnp.where(tags == s, local[s].astype(F32), tag)
    told[...] = tag[0:8]
    c_ref[q] = xv[...]

    pl.semaphore_wait(barrier, 7 + NY - 1 + NZ - 1 + jnp.where(fixed, 0, 1))

    sends = []

    def send(*args):
        copy = rcopy(*args)
        copy.start()
        sends.append(copy)

    piece = xv.at[:, W:OWN]
    mine = xv
    out = rcopy(piece, g_ref.at[half * NCOL + q], ps.at[0], pr.at[0], swap)
    keep = pltpu.make_async_copy(piece, g_ref.at[p], lsem.at[0])
    out_tag = rcopy(told, heard.at[0], ps.at[1], pr.at[1], swap)
    keep_tag = pltpu.make_async_copy(told, heard.at[0], lsem.at[1])

    @pl.when(jnp.logical_not(fixed))
    def _():
        out.start()
        out_tag.start()

    @pl.when(fixed)
    def _():
        keep.start()
        keep_tag.start()

    def ring(a, t, src_up, src_down):
        zz = zh if a == 0 else 1 - zh
        if src_up is not None:
            at = zz * NY + (y + NY - t) % NY
            send(src_up, c_ref.at[at], cus.at[a * 4 + t], cur.at[a * 4 + t], up)
        if src_down is not None:
            at = zz * NY + (y + t) % NY
            send(src_down, c_ref.at[at], cds.at[a * 4 + t], cdr.at[a * 4 + t], down)

    def ring_up_wait(a, t):
        zz = zh if a == 0 else 1 - zh
        got = c_ref.at[zz * NY + (y + NY - 1 - t) % NY]
        rcopy(got, got, cus.at[a * 4 + t], cur.at[a * 4 + t], up).wait_recv()
        if t + 1 < UPS[a]:
            ring(a, t + 1, got, None)

    def ring_down_wait(a, t):
        zz = zh if a == 0 else 1 - zh
        got = c_ref.at[zz * NY + (y + 1 + t) % NY]
        rcopy(got, got, cds.at[a * 4 + t], cdr.at[a * 4 + t], down).wait_recv()
        if t + 1 < DOWNS[a]:
            ring(a, t + 1, None, got)

    send(mine, c_ref.at[q], chs.at[0], chr_.at[0], far)
    ring(0, 0, mine, mine)

    load_s.wait()
    for s in range(SL):
        for c in range(8):
            blocks = [sv[pl.ds(r * B * 8 + c, B, stride=8), :] for r in range(RC)]
            sub8[s * B : (s + 1) * B, c * B : (c + 1) * B] = pick(blocks, local[s])

    def ring_wait(a, t):
        if t < UPS[a]:
            ring_up_wait(a, t)
        if t < DOWNS[a]:
            ring_down_wait(a, t)

    ring_wait(0, 0)
    ring_wait(0, 1)
    other = c_ref.at[(1 - zh) * NY + y]
    rcopy(other, other, chs.at[0], chr_.at[0], far).wait_recv()
    ring(1, 0, other, other)

    @pl.when(jnp.logical_not(fixed))
    def _():
        rcopy(piece, g_ref.at[p], ps.at[0], pr.at[0], swap).wait_recv()
        out_tag.wait_recv()

    @pl.when(fixed)
    def _():
        keep.wait()
        keep_tag.wait()

    def fan(src, dz):
        got = g_ref.at[src]
        for d in (2, 1, 3) if dz == 2 else (1, 3):
            send(got, got, gxs.at[dz * 3 + d - 1], gxr.at[dz * 3 + d - 1], xk[d, 0])
        send(got, got, gks.at[dz * 4], gkr.at[dz * 4], core)

    own = g_ref.at[p]
    for d in (1, 3, 2):
        send(own, own, gzs.at[d - 1], gzr.at[d - 1], lzdev[d])
    fan(p, 0)
    send(heard.at[0], heard.at[1], gxs.at[12], gxr.at[12], xk[2, 0])

    def z_wait(d):
        src = row_id(x, (zl + NZL - d) % NZL, k)
        got = g_ref.at[src]
        rcopy(got, got, gzs.at[d - 1], gzr.at[d - 1], lzdev[d]).wait_recv()
        fan(src, d)

    def x_wait(dz, d):
        src = row_id((x + NX - d) % NX, (zl + NZL - dz) % NZL, k)
        got = g_ref.at[src]
        n = dz * 3 + d - 1
        rcopy(got, got, gxs.at[n], gxr.at[n], xk[d, 0]).wait_recv()
        n = dz * 3 + 1
        if (dz, d) in ((0, 1), (1, 3), (3, 3)):
            send(got, got, gxs.at[n], gxr.at[n], xk[d, 0])
        send(got, got, gks.at[dz * 4 + d], gkr.at[dz * 4 + d], core)

    ring_wait(0, 2)
    z_wait(1)
    z_wait(3)
    x_wait(0, 1)
    x_wait(0, 3)
    ring_wait(1, 0)
    z_wait(2)
    x_wait(0, 2)
    ring_wait(0, 3)
    x_wait(1, 1)
    x_wait(1, 3)
    ring_wait(1, 1)
    x_wait(3, 1)
    x_wait(3, 3)
    x_wait(1, 2)
    x_wait(3, 2)
    x_wait(2, 1)
    x_wait(2, 3)
    ring_wait(1, 2)
    x_wait(2, 2)

    rcopy(heard.at[1], heard.at[1], gxs.at[12], gxr.at[12], xk[2, 0]).wait_recv()
    said = [[jnp.max(jnp.where(tags[0:8] == t, heard[h], 0.0)) for t in range(SL)] for h in range(2)]
    for h in range(2):
        for t in range(SL):
            which = jnp.where(half == h, said[0][t], said[1][t])
            for s in range(SL):
                at = slice(s * B, (s + 1) * B)
                n = h * SL + t
                value = sub8[at, h * B : (h + 1) * B]
                for r in range(1, RC):
                    block = sub8[at, (2 * r + h) * B : (2 * r + h + 1) * B]
                    value = jnp.where(which > r - 0.5, block, value)
                sub[at, n * B : (n + 1) * B] = value

    for dz in (0, 1, 3, 2):
        for d in (0, 1, 3, 2):
            src = row_id((x + NX - d) % NX, (zl + NZL - dz) % NZL, 1 - k)
            got = g_ref.at[src]
            rcopy(got, got, gks.at[dz * 4 + d], gkr.at[dz * 4 + d], core).wait_recv()

    def panel(h, at):
        return halves(g_ref[h * NCOL : (h + 1) * NCOL, :, at : at + ROWS].reshape(W, ROWS))

    gp = [panel(h, 0) for h in range(2)]
    gq = [panel(h, ROWS) for h in range(2)]
    for s in range(SL):
        at = slice(s * B, (s + 1) * B)
        left = [halves(sub[at, h * ROWS : (h + 1) * ROWS]) for h in range(2)]
        yv[at, :] = dot3(left[0], gp[0], NT) + dot3(left[1], gp[1], NT)
        zv[at, :] = dot3(left[0], gq[0], NT) + dot3(left[1], gq[1], NT)
    ring_wait(1, 3)
    topf = c_ref[:, :, 0:W].reshape(W, W)
    top = halves(topf)
    rows = lax.broadcasted_iota(jnp.int32, (B, 1), 0)
    for s in range(SL):
        at = slice(s * B, (s + 1) * B)
        yy = jnp.where(rows < psz[s], -yv[at, :], 0.0)
        zz = jnp.where(rows < csz[s], -(zv[at, :] + dot3(halves(yy), top, NN)), 0.0)
        yv[at, :] = yy
        zv[at, :] = zz
        yz[:, :, s * CB : (s + 1) * CB, 0:W] = yy.reshape(NZH, NY, CB, W)
        yz[:, :, s * CB : (s + 1) * CB, W : 2 * W] = zz.reshape(NZH, NY, CB, W)

    def sum_up(a, t):
        n = a * 4 + t
        dst = ubuf.at[n]
        if t == 0:
            src = yz.at[a, (y + UPS[a]) % NY]
        else:
            src = ubuf.at[n - 1]
            rcopy(src, src, us.at[n - 1], ur.at[n - 1], up).wait_recv()
            ubuf[n - 1] = ubuf[n - 1] + yz[a, (y + UPS[a] - t) % NY]
        send(src, dst, us.at[n], ur.at[n], up)

    def sum_down(a, t):
        n = a * 4 + t
        dst = dbuf.at[n]
        if t == 0:
            src = yz.at[a, (y + NY - DOWNS[a]) % NY]
        else:
            src = dbuf.at[n - 1]
            rcopy(src, src, ds.at[n - 1], dr.at[n - 1], down).wait_recv()
            dbuf[n - 1] = dbuf[n - 1] + yz[a, (y + NY - DOWNS[a] + t) % NY]
        send(src, dst, ds.at[n], dr.at[n], down)

    def sum_step(t):
        for a in range(2):
            if t < UPS[a]:
                sum_up(a, t)
            if t < DOWNS[a]:
                sum_down(a, t)

    sum_step(0)

    def put(m, mat):
        for n in range(2):
            aue[n, m] = mat[:, n * 128 : (n + 1) * 128]
        send(aue.at[1 - k, m], kbuf.at[m], ks.at[m], kr.at[m], core)

    pp = halves(c_ref[:, :, W : W + ROWS].reshape(W, ROWS))
    qp = halves(c_ref[:, :, W + ROWS : OWN].reshape(W, ROWS))
    ysp = halves(yv[...])
    a_mat = dot3(pp, ysp, NN)
    put(0, a_mat)
    uv[...] = dot3(halves(a_mat), top, NN) - dot3(qp, ysp, NN).T
    first = jnp.where(p == 0, 1.0, 0.0)
    mid = pl.ds(pl.multiple_of(q * SHARE, SHARE), SHARE)
    uv[mid, :] = uv[mid, :] - first * dot3(halves(d_ref[...]), top, NN)
    u_mat = uv[...]
    put(1, u_mat)
    e_mat = -dot3(halves(topf.T), halves(u_mat), NN) - dot3(qp, halves(zv[...]), NN)
    put(2, e_mat)

    busy = x < 3
    ahead, behind = xk[1, 0], xk[3, 0]
    nxt, prv = (x + 1) % NX, (x + 3) % NX

    def xcopy(n, m, part, dev):
        return rcopy(acc.at[m, part], xbuf.at[n], xs.at[n], xr.at[n], dev)

    def landed(n, dev):
        rcopy(xbuf.at[n], xbuf.at[n], xs.at[n], xr.at[n], dev).wait_recv()

    def relay_up():
        return xcopy(0, (x + 2) % NX, 1, ahead)

    def relay_down():
        return xcopy(1, (x + 2) % NX, 0, behind)

    def plain_up():
        return xcopy(2, nxt, 0, ahead)

    def plain_down():
        return xcopy(3, prv, 1, behind)

    def total_up():
        return xcopy(4, nxt, 1, ahead)

    def total_down():
        return xcopy(5, prv, 0, behind)

    def merge(m):
        got = kbuf.at[m]
        rcopy(got, got, ks.at[m], kr.at[m], core).wait_recv()
        acc[m] = (aue[k, m] + kbuf[m]).reshape(2, 128, 128)

    opposite = (x + 2) % NX

    @pl.when(opposite < 3)
    def _():
        merge(opposite)
        relay_up().start()
        relay_down().start()

    @pl.when(nxt < 3)
    def _():
        merge(nxt)
        plain_up().start()

    @pl.when(prv < 3)
    def _():
        merge(prv)
        plain_down().start()

    @pl.when(busy)
    def _():
        merge(x)

    sum_step(1)

    @pl.when(nxt < 3)
    def _():
        landed(0, ahead)
        acc[nxt, 1] = acc[nxt, 1] + xbuf[0]
        total_up().start()

    @pl.when(prv < 3)
    def _():
        landed(1, behind)
        acc[prv, 0] = acc[prv, 0] + xbuf[1]
        total_down().start()

    sum_step(2)

    def ycopy(d):
        return rcopy(accx.at[:, (y + d) % NY], ybuf.at[d - 1], ys.at[d - 1], yr.at[d - 1], ydev[d])

    def zcopy(d):
        return rcopy(accy.at[zpos[d] // NZL], zbuf.at[d - 1], zs.at[d - 1], zr.at[d - 1], zdev[d])

    def fcopy(d, f):
        n = d * 2 + f - 1
        return rcopy(auo.at[x, k], auo.at[x, k], fs.at[n], fr.at[n], xk[d, f])

    @pl.when(busy)
    def _():
        for n in range(2, 6):
            landed(n, ahead if n % 2 == 0 else behind)
        low = acc[x, 0] + (xbuf[2] + xbuf[5])
        high = acc[x, 1] + (xbuf[3] + xbuf[4])
        accx[0] = low.reshape(NY, SHARE, 128)
        accx[1] = high.reshape(NY, SHARE, 128)
        for d in (4, 3, 5, 2, 6, 1, 7):
            ycopy(d).start()

    sum_step(3)
    for a in range(2):
        n = a * 4 + UPS[a] - 1
        got = ubuf.at[n]
        rcopy(got, got, us.at[n], ur.at[n], up).wait_recv()
        n2 = a * 4 + DOWNS[a] - 1
        got = dbuf.at[n2]
        rcopy(got, got, ds.at[n2], dr.at[n2], down).wait_recv()
        yzacc[a] = yz[a, y] + (ubuf[n] + dbuf[n2])
    send(yzacc.at[1 - zh], hbuf, hs.at[0], hr.at[0], far)

    hop = rcopy(hbuf, hbuf, hs.at[0], hr.at[0], far)
    @pl.when(busy)
    def _():
        for d in range(1, NY):
            ycopy(d).wait_recv()
        total = accx[:, y]
        for d in range(NY - 1):
            total = total + ybuf[d]
        accy[...] = total
        for d in (4, 3, 5, 2, 6, 1, 7):
            zcopy(d).start()

    hop.wait_recv()
    yzo[...] = yzacc[zh] + hbuf[...]

    @pl.when(busy)
    def _():
        for d in range(1, NZ):
            zcopy(d).wait_recv()
        total = accy[zh]
        for d in range(NZ - 1):
            total = total + zbuf[d]
        auo[x, k] = total
        for d, f in xk:
            fcopy(d, f).start()

    for d, f in xk:
        m = (x + NX - d) % NX
        n = d * 2 + f - 1

        @pl.when(m < 3)
        def _():
            got = auo.at[m, k if f == 0 else 1 - k]
            rcopy(got, got, fs.at[n], fr.at[n], xk[d, f]).wait_recv()

    @pl.when(jnp.logical_not(fixed))
    def _():
        out.wait_send()
        out_tag.wait_send()

    for copy in sends:
        copy.wait_send()

    @pl.when((x + 2) % NX < 3)
    def _():
        relay_up().wait_send()
        relay_down().wait_send()

    @pl.when(nxt < 3)
    def _():
        plain_up().wait_send()
        total_up().wait_send()

    @pl.when(prv < 3)
    def _():
        plain_down().wait_send()
        total_down().wait_send()

    @pl.when(busy)
    def _():
        for d in range(1, NY):
            ycopy(d).wait_send()
        for d in range(1, NZ):
            zcopy(d).wait_send()
        for d, f in xk:
            fcopy(d, f).wait_send()


def step(*operands):
    vmem = pl.BlockSpec(memory_space=pltpu.VMEM)
    dma = pltpu.SemaphoreType.DMA
    rows = SL * CB
    buffers = [
        (SL, SHARE, B),
        (SL, SHARE, B),
        (SHARE, W),
        (RC * B * 8, B),
        (ROWS, 8 * B),
        (ROWS, 2 * ROWS),
        (SHARE, OWN),
        (8, 128),
        (2, 8, 128),
        (NROW, SHARE, PATCH),
        (NCOL, SHARE, OWN),
        (ROWS, W),
        (ROWS, W),
        (W, W),
        (NZH, NY, rows, 2 * W),
        (2, 3, W, 128),
        (3, W, 128),
        (3, 2, 128, 128),
        (6, 128, 128),
        (NZH, NY, SHARE, 128),
        (NY - 1, NZH, SHARE, 128),
        (NZH, SHARE, 128),
        (NZ - 1, SHARE, 128),
        (8, rows, 2 * W),
        (8, rows, 2 * W),
        (NZH, rows, 2 * W),
        (rows, 2 * W),
    ]
    sems = [1, 7, 2, 2, 2, 3, 3, 13, 13, 16, 16, 1, 1, 8, 8, 8, 8]
    sems += [3, 3, 6, 6, 7, 7, 7, 7, 7, 7, 8, 8, 8, 8, 1, 1]
    return pl.pallas_call(
        step_kernel,
        out_shape=(
            jax.ShapeDtypeStruct((rows, 2 * W), F32),
            jax.ShapeDtypeStruct((3, 2, SHARE, 128), F32),
        ),
        in_specs=[pl.BlockSpec(memory_space=pl.ANY)] * 8,
        out_specs=(vmem, vmem),
        scratch_shapes=[pltpu.SMEM((SL,), jnp.int32)] * 3
        + [pltpu.VMEM(b, F32) for b in buffers]
        + [dma((n,)) for n in sems],
        compiler_params=pltpu.CompilerParams(collective_id=0, has_side_effects=True),
        name="step",
    )(*operands)


def place_kernel(pb, yz_ref, mats_ref, d_ref, cd_ref, prow, pd, crow, cu, cdiag):
    p = lax.axis_index("row")
    for r in range(RC):
        ya = jnp.zeros((CB, W), F32)
        za = jnp.zeros((CB, W), F32)
        for s in range(SL):
            here = pb[s] == r * NROW + p
            ya = jnp.where(here, yz_ref[s * CB : (s + 1) * CB, 0:W], ya)
            za = jnp.where(here, yz_ref[s * CB : (s + 1) * CB, W:], za)
        prow[r] = ya
        crow[r] = za
    for n in range(2):
        at = slice(n * 128, (n + 1) * 128)
        pd[:, at] = d_ref[:, at] - mats_ref[0, n]
        cu[:, at] = mats_ref[1, n]
        cdiag[:, at] = cd_ref[:, at] + mats_ref[2, n]


def lay(*operands):
    vmem = pl.BlockSpec(memory_space=pltpu.VMEM)
    smem = pl.BlockSpec(memory_space=pltpu.SMEM)
    share = jax.ShapeDtypeStruct((SHARE, W), F32)
    rows = jax.ShapeDtypeStruct((RC, CB, W), F32)
    return pl.pallas_call(
        place_kernel,
        out_shape=(rows, share, rows, share, share),
        in_specs=[smem] + [vmem] * 4,
        out_specs=(vmem,) * 5,
        name="lay",
    )(*operands)


def body(
    cached_inverse,
    parent_panel,
    parent_blocks,
    parent_sizes,
    parent_diagonal,
    child_panel,
    child_top,
    child_blocks,
    child_sizes,
    child_diagonal,
):
    rows, mats = step(
        parent_blocks,
        parent_sizes,
        child_sizes,
        cached_inverse.reshape(RC * B * 8, B),
        jnp.transpose(parent_panel, (1, 0, 2)),
        jnp.transpose(child_panel, (1, 0, 2)),
        child_top,
        parent_diagonal,
    )
    prow, pd, crow, cu, cdiag = lay(parent_blocks, rows, mats, parent_diagonal, child_diagonal)
    return (prow[:, None], pd, crow[:, None], cu, cdiag)


def solution(mesh):
    in_specs = (
        P(None, "row", None, None, "col", None),
        P("col", "row", None),
        P("row"),
        P("row"),
        P("col", None),
        P("col", "row", None),
        P("col", None),
        P("row"),
        P("row"),
        P("col", None),
    )
    out_specs = (
        P(None, "row", "col", None),
        P("col", None),
        P(None, "row", "col", None),
        P("col", None),
        P("col", None),
    )
    return jax.shard_map(body, mesh=mesh, in_specs=in_specs, out_specs=out_specs, check_vma=False)
```
